256 devices in a mesh: dp: 8 (over x, y_hi), tensor: 32 (over y_lo, z, core).
Axes of the slice: x: 4, y: 4 (y_hi: 2, y_lo: 2; y = y_hi * 2 + y_lo), z: 8, core: 2. Of those that a mesh axis runs over, the one named last changes fastest.
Arguments:
- query_states: bfloat16 [3072, 4096], P('dp', 'tensor'), may hold values from -64 to 64
- key_states: bfloat16 [3072, 4096], P('dp', 'tensor'), may hold values from -12 to 12
- value_states: bfloat16 [3072, 4096], P('dp', 'tensor'), may hold values from -6 to 6
- residual: bfloat16 [3072, 4096], P('dp', 'tensor'), may hold values from -6 to 6
- norm_gains: float32 [4, 4096], replicated, may hold values from 0.1 to 1.9
- lang_labels: int32 [64], replicated, may hold values from 0 to 3
- doc_lengths: int32 [64, 4], replicated, may hold values from 1 to 32, 48 in all within a row
- destinations: int32 [64], replicated, may hold values from 0 to 7, as said below
- gate_weight: bfloat16 [4096, 14336], P(None, 'tensor'), may hold values from -0.09375 to 0.09375
- up_weight: bfloat16 [4096, 14336], P(None, 'tensor'), may hold values from -0.09375 to 0.09375
- down_weight: bfloat16 [14336, 4096], P('tensor'), may hold values from -0.046875 to 0.046875
- out_cotangent: bfloat16 [3072, 4096], P(('dp', 'tensor')), may hold values from -6 to 6
Outputs:
- layer_out: bfloat16 [3072, 4096], P(('dp', 'tensor'))
- input_grad: bfloat16 [3072, 4096], P(('dp', 'tensor'))
- gate_grad: bfloat16 [4096, 14336], P('dp', 'tensor')
- up_grad: bfloat16 [4096, 14336], P('dp', 'tensor')
- down_grad: bfloat16 [14336, 4096], P('tensor', 'dp')
The draws below stay inside these ranges and needn't reach their ends.
Inputs may be any that keep to these rules, and one draw needn't show every extreme that they name: `destinations`: every data group receives exactly 8 units. One group sends at most 2 units to any one group, and every group sends exactly 2 units to some group.
All inputs are finite; a program needn't handle non-finite values.
Results may differ from the reference program's by a relative error of at most 0.015.
Values may be sent and summed in bfloat16 or wider, within the bound.
No kernel may reach another device: no remote copies, remote signals or barrier semaphores. Data moves between devices by JAX's collectives and lax.ppermute only.
A program may use at most 128 MiB of HBM per device.

```python
import math
import jax
import jax.numpy as jnp
import numpy as np
from jax import lax

D = 4096
FF = 14336
HEADS = 32
HD = 128
UNIT = 48
UNITS = 8
CAP = 2
NDOC = 4
NLANG = 4
MOST = 32
WIN = 24
TOK_GRP = 384
NUNITS = 64
TOK_ALL = 3072
N_DP = 8


def drawn_pair(key):
    base_key = jax.random.fold_in(key, 101)
    key_noise, query_noise = jax.random.split(base_key, 2)
    array_shape = (TOK_ALL, D)
    keys_drawn = jnp.clip(jax.random.normal(key_noise, array_shape, jnp.float32), -6.0, 6.0)
    queries_drawn = jnp.clip(jax.random.normal(query_noise, array_shape, jnp.float32), -6.0, 6.0)
    queries = queries_drawn
    keys_out = keys_drawn
    return (jnp.clip(queries, -64.0, 64.0), jnp.clip(keys_out, -12.0, 12.0))


def draw_query_states(key, part):
    return drawn_pair(key)[0].astype(jnp.bfloat16)


def draw_key_states(key, part):
    return drawn_pair(key)[1].astype(jnp.bfloat16)


def draw_destinations(key, part):
    base_key = jax.random.fold_in(key, 202)
    offset_key, shuffle_key = jax.random.split(base_key)
    shuffled = jax.random.permutation(offset_key, N_DP)
    offsets = shuffled[jnp.arange(UNITS) // CAP]

    def per_group(group_index):
        unit_order = jax.random.permutation(jax.random.fold_in(shuffle_key, group_index), UNITS)
        return (group_index + offsets[unit_order]) % N_DP
    return jax.vmap(per_group)(jnp.arange(N_DP, dtype=jnp.int32)).reshape(-1).astype(jnp.int32)


def place_ends(values, rng, least, top_value):
    index_at = [jax.random.randint(jax.random.fold_in(rng, axis), (), 0, length) for axis, length in enumerate(values.shape)]
    widest = values.shape.index(max(values.shape))
    beside = index_at[:widest] + [(index_at[widest] + 1) % values.shape[widest]] + index_at[widest + 1:]
    return values.at[tuple(index_at)].set(least).at[tuple(beside)].set(top_value)


def block_levels(own_key, extent, cuts, low, largest):
    loudness = 1.0
    for axis_at, blocks in cuts:
        draws = jax.random.uniform(jax.random.fold_in(jax.random.fold_in(own_key, 6), axis_at), (blocks,), jnp.float32, low / len(cuts), largest / len(cuts))
        loudness = loudness * jnp.repeat(jnp.exp(draws), extent[axis_at] // blocks).reshape((-1,) + (1,) * (len(extent) - 1 - axis_at))
    return loudness


def profile(number_of, total, bound, lean):
    weights = [(1 << 20) // math.isqrt(grade ** lean) + 1 for grade in range(2, number_of + 1)]
    surplus, counts = total - bound - (number_of - 1), [1] * (number_of - 1)
    while surplus > 0:
        movable = [i for i in range(number_of - 1) if counts[i] < bound]
        mass, budget = sum([weights[i] for i in movable]), surplus
        for i in movable:
            more = min(bound - counts[i], max(1, budget * weights[i] // mass), surplus)
            counts[i] = counts[i] + more
            surplus = surplus - more
    return np.array([bound] + counts)


def uneven(rng, count, total, bound, skew):
    if count == 2:
        one = jax.random.randint(rng, (), max(1, total - bound), min(bound, total - 1) + 1)
        return jnp.stack([one, total - one])
    tallies = jnp.asarray(profile(count, total, bound, skew), jnp.int32)
    twos = (count - 1) // 2
    source_of, receiver = tallies[1:1 + 2 * twos:2], tallies[2:2 + 2 * twos:2]
    slack = jnp.minimum(source_of - 1, bound - receiver)
    moved = jax.random.randint(jax.random.fold_in(rng, 1), (twos,), 0, 1 << 20) % (slack + 1)
    tallies = tallies.at[1:1 + 2 * twos:2].set(source_of - moved).at[2:2 + 2 * twos:2].set(receiver + moved)
    return tallies[jax.random.permutation(jax.random.fold_in(rng, 2), count)]


def gaussian(stream_key, shape, width, most, cuts=(), kind=jnp.bfloat16):
    result = width * jax.random.normal(stream_key, shape, jnp.float32)
    if cuts:
        result = result * block_levels(stream_key, shape, cuts, -0.22, 0.18)
    return jnp.clip(result, -most, most).astype(kind)


def setup_inputs(seed: int = 0) -> dict:
    arg_keys = jax.random.split(jax.random.key(seed), 13)
    return {
        "query_states": draw_query_states(jax.random.fold_in(arg_keys[12], 71), 0),
        "key_states": draw_key_states(jax.random.fold_in(arg_keys[12], 71), 0),
        "value_states": gaussian(arg_keys[2], (TOK_ALL, D), 1.0, 6.0, ((0, 8), (1, 32))),
        "residual": gaussian(arg_keys[3], (TOK_ALL, D), 1.0, 6.0, ((0, 8), (1, 32))),
        "norm_gains": jnp.clip(1.0 + 0.18 * jax.random.normal(arg_keys[4], (NLANG, D), jnp.float32), 0.1, 1.9),
        "lang_labels": place_ends(jax.random.randint(arg_keys[5], (NUNITS,), 0, NLANG), jax.random.fold_in(arg_keys[5], 1), 0, NLANG - 1).astype(jnp.int32),
        "doc_lengths": jax.vmap(lambda own: uneven(own, NDOC, UNIT, MOST, 2))(jax.random.split(arg_keys[6], NUNITS)).reshape((NUNITS, NDOC)).astype(jnp.int32),
        "destinations": draw_destinations(jax.random.fold_in(arg_keys[12], 71), 0),
        "gate_weight": gaussian(arg_keys[8], (D, FF), D ** -0.5, 0.09375, ((1, 32),)),
        "up_weight": gaussian(arg_keys[9], (D, FF), D ** -0.5, 0.09375, ((1, 32),)),
        "down_weight": gaussian(arg_keys[10], (FF, D), FF ** -0.5, 0.046875, ((0, 32),)),
        "out_cotangent": gaussian(arg_keys[11], (TOK_ALL, D), 1.0, 6.0, ((0, 256),)),
    }


def doc_index(doc_lengths):
    doc_ends = jnp.cumsum(doc_lengths, axis=1)
    positions = jnp.arange(UNIT, dtype=jnp.int32)
    return lax.optimization_barrier(jnp.sum((doc_ends[:, None, :] <= positions[None, :, None]).astype(jnp.int32), axis=2))

def attend(query_units, key_units, value_units, resid_units, doc_units):
    unit_count = query_units.shape[0]
    head_shape = (unit_count, UNIT, HEADS, HD)
    query_heads = query_units.reshape(head_shape).astype(jnp.float32)
    key_heads = key_units.reshape(head_shape).astype(jnp.float32)
    value_heads = value_units.reshape(head_shape).astype(jnp.float32)
    scores = jnp.einsum('uqhd,ukhd->uhqk', query_heads, key_heads) / math.sqrt(HD)
    positions = jnp.arange(UNIT, dtype=jnp.int32)
    distance = positions[:, None] - positions[None, :]
    allowed = (doc_units[:, :, None] == doc_units[:, None, :]) & ((distance >= 0) & (distance < WIN))[None]
    scores = jnp.where(allowed[:, None], scores, -1e+30)
    row_max = lax.optimization_barrier(jnp.max(scores, axis=3, keepdims=True))
    exp_scores = jnp.exp(scores - row_max)
    attn_probs = (exp_scores / lax.optimization_barrier(jnp.sum(exp_scores, axis=3, keepdims=True))).astype(jnp.bfloat16)
    mixed_heads = jnp.einsum('uhqk,ukhd->uqhd', attn_probs.astype(jnp.float32), value_heads)
    return (resid_units.astype(jnp.float32) + mixed_heads.reshape(unit_count, UNIT, D)).astype(jnp.bfloat16)

def reference(query_states, key_states, value_states, residual, norm_gains, lang_labels, doc_lengths, destinations, gate_weight, up_weight, down_weight, out_cotangent):
    unit_shape = (NUNITS, UNIT, D)
    doc_ids = doc_index(doc_lengths)
    mixed = attend(query_states.reshape(unit_shape), key_states.reshape(unit_shape), value_states.reshape(unit_shape), residual.reshape(unit_shape), doc_ids)
    unit_order = jnp.argsort(destinations, stable=True).astype(jnp.int32)
    stream = mixed[unit_order].reshape(TOK_ALL, D)
    lang_units = lang_labels[unit_order]
    gain_tokens = jnp.repeat(norm_gains[lang_units], UNIT, axis=0)
    stream_f = stream.astype(jnp.float32)
    scaled = (stream_f * gain_tokens).astype(jnp.bfloat16)
    inv_rms = lax.rsqrt(lax.optimization_barrier(jnp.sum(stream_f * stream_f, axis=1)) / D + 1e-05)
    act_gate = inv_rms[:, None] * jnp.dot(scaled, gate_weight, preferred_element_type=jnp.float32)
    act_up = inv_rms[:, None] * jnp.dot(scaled, up_weight, preferred_element_type=jnp.float32)
    hidden = (jax.nn.silu(act_gate) * act_up).astype(jnp.bfloat16)
    layer_out = (stream_f + jnp.dot(hidden, down_weight, preferred_element_type=jnp.float32)).astype(jnp.bfloat16)
    grad_hidden = jnp.dot(out_cotangent, down_weight.T, preferred_element_type=jnp.float32)
    sigma = jax.nn.sigmoid(act_gate)
    grad_gate = (inv_rms[:, None] * grad_hidden * act_up * sigma * (1.0 + act_gate * (1.0 - sigma))).astype(jnp.bfloat16)
    grad_up = (inv_rms[:, None] * grad_hidden * jax.nn.silu(act_gate)).astype(jnp.bfloat16)
    back = jnp.dot(grad_gate, gate_weight.T, preferred_element_type=jnp.float32) + jnp.dot(grad_up, up_weight.T, preferred_element_type=jnp.float32)
    dot_sum = lax.optimization_barrier(jnp.sum(scaled.astype(jnp.float32) * back, axis=1))
    input_grad = (out_cotangent.astype(jnp.float32) + gain_tokens * back - (inv_rms * inv_rms / D)[:, None] * stream_f * dot_sum[:, None]).astype(jnp.bfloat16)
    factors = jnp.concatenate([grad_gate, grad_up], axis=1)

    def group_terms(totals, group_index):
        row_start = group_index * TOK_GRP
        scaled_rows = lax.dynamic_slice_in_dim(scaled, row_start, TOK_GRP, 0)
        factor_rows = lax.dynamic_slice_in_dim(factors, row_start, TOK_GRP, 0)
        hidden_rows = lax.dynamic_slice_in_dim(hidden, row_start, TOK_GRP, 0)
        cot_rows = lax.dynamic_slice_in_dim(out_cotangent, row_start, TOK_GRP, 0)
        gate_up_part = jnp.dot(scaled_rows.T, factor_rows, preferred_element_type=jnp.float32).astype(jnp.bfloat16)
        down_part = jnp.dot(cot_rows.T, hidden_rows, preferred_element_type=jnp.float32).astype(jnp.bfloat16)
        gate_up_part, down_part = lax.optimization_barrier((gate_up_part, down_part))
        return ((totals[0] + gate_up_part.astype(jnp.float32), totals[1] + down_part.astype(jnp.float32)), None)
    start_totals = (jnp.zeros((D, 2 * FF), jnp.float32), jnp.zeros((D, FF), jnp.float32))
    group_ids = jnp.arange(N_DP, dtype=jnp.int32)
    totals, unused = lax.scan(group_terms, start_totals, group_ids)
    gate_grad = totals[0][:, :FF].astype(jnp.bfloat16)
    up_grad = totals[0][:, FF:].astype(jnp.bfloat16)
    down_grad = totals[1].T.astype(jnp.bfloat16)
    return (layer_out, input_grad, gate_grad, up_grad, down_grad)
```

```python
import math

import jax
import jax.numpy as jnp
from jax import lax
from jax.sharding import Mesh
from jax.sharding import PartitionSpec as P

UNIT = 48
CAP = 2
WIN = 24
DP = ("x", "yh")
TENSOR = ("yl", "z", "c")
DP_TENSOR = ("x", "yh", "yl", "z", "c")
F32 = jnp.float32
BF16 = jnp.bfloat16


def moved(array, axis, step):
    n = lax.axis_size(axis)
    return lax.ppermute(array, axis, [(i, (i + step) % n) for i in range(n)])


def joined(mine, other, index, dim):
    return jnp.where(
        index == 0,
        jnp.concatenate([mine, other], axis=dim),
        jnp.concatenate([other, mine], axis=dim),
    )


def ring_order(pieces, index):
    n = len(pieces)
    stack = jnp.stack(pieces)
    twice = jnp.concatenate([stack, stack], axis=0)
    return lax.dynamic_slice_in_dim(twice, (n - index) % n, n, 0)


def gathered_over_z(piece):
    n = lax.axis_size("z")
    pieces = [piece] * n
    for r in sorted(range(1, n), key=lambda r: -min(r, n - r)):
        pieces[r] = moved(piece, "z", -r)
    return ring_order(pieces, lax.axis_index("z"))


def part_of(array, index, size, dim):
    return lax.dynamic_slice_in_dim(array, index * size, size, dim)


def doc_index(doc_lengths, unit_len):
    doc_ends = jnp.cumsum(doc_lengths, axis=1)
    positions = jnp.arange(unit_len, dtype=jnp.int32)
    return jnp.sum((doc_ends[:, None, :] <= positions[None, :, None]).astype(jnp.int32), axis=2)


def attend(query_units, key_units, value_units, resid_units, doc_units):
    head = query_units.shape[2]
    scores = jnp.einsum(
        "uqd,ukd->uqk", query_units, key_units, preferred_element_type=F32
    ) / math.sqrt(head)
    positions = jnp.arange(query_units.shape[1], dtype=jnp.int32)
    distance = positions[:, None] - positions[None, :]
    allowed = (doc_units[:, :, None] == doc_units[:, None, :]) & (
        (distance >= 0) & (distance < WIN)
    )[None]
    scores = jnp.where(allowed, scores, -1e30)
    row_max = jnp.max(scores, axis=2, keepdims=True)
    exp_scores = jnp.exp(scores - row_max)
    attn_probs = (exp_scores / jnp.sum(exp_scores, axis=2, keepdims=True)).astype(BF16)
    mixed = jnp.einsum("uqk,ukd->uqd", attn_probs, value_units, preferred_element_type=F32)
    return (resid_units.astype(F32) + mixed).astype(BF16)


def column_blocks(full, width):
    x, c = lax.axis_index("x"), lax.axis_index("c")
    n = lax.axis_size("x")

    def block(s, core):
        return part_of(full, 2 * ((x + s) % n) + core, width, 1)

    below = moved(block(1, c), "x", 1)
    above = moved(block(n - 1, c), "x", -1)
    across = moved(block(2, c), "x", 2)
    got = jnp.stack([above, below, across])
    other = moved(got, "c", 1)
    mine = jnp.concatenate([block(0, c), above, below, across], axis=0)
    theirs = jnp.concatenate([block(0, 1 - c), other[0], other[1], other[2]], axis=0)
    same = c == lax.axis_index("yh")
    return jnp.where(same, mine, theirs), jnp.where(same, theirs, mine)


def gathered_over_x(factor):
    half = factor.shape[0] // 2
    below = moved(factor, "x", 1)
    above = moved(factor, "x", -1)
    upper = moved(below[:half], "x", 1)
    lower = moved(above[half:], "x", -1)
    across = jnp.concatenate([upper, lower], axis=0)
    return jnp.concatenate([factor, above, below, across], axis=1)


def weight_grad(factor_all, blocks):
    keep, send = blocks
    sent = jnp.dot(factor_all, send, preferred_element_type=F32).astype(BF16)
    arrived = moved(sent, "yh", 1)
    kept = jnp.dot(factor_all, keep, preferred_element_type=F32)
    return (kept + arrived.astype(F32)).astype(BF16)


def row_sums(part, rows_here):
    c, z, yl = lax.axis_index("c"), lax.axis_index("z"), lax.axis_index("yl")
    n = lax.axis_size("z")
    half = part.shape[1] // 2
    chip = 2 * rows_here
    shape = (2, n, chip, half)
    sent = part_of(part, 1 - c, half, 1)
    kept = part_of(part, c, half, 1).reshape(shape)
    arrived = moved(sent, "c", 1).reshape(shape)

    def own(r):
        at = (z + r) % n
        pick = lambda a: lax.dynamic_slice_in_dim(a, at, 1, 1)[:, 0].astype(F32)
        return pick(kept) + pick(arrived)

    far = own(n // 2).astype(BF16)
    up = moved(far[0], "z", 1)
    down = moved(far[1], "z", -1)
    near = own(n // 2 - 1)
    up = jnp.stack([near[0] + up.astype(F32), near[1]])
    near = own(n - n // 2 + 1)
    down = jnp.stack([near[0], near[1] + down.astype(F32)])
    for r in range(n // 2 - 2, -1, -1):
        up = moved(up.astype(BF16), "z", 1)
        down = moved(down.astype(BF16), "z", -1)
        if r:
            up = own(r) + up.astype(F32)
            down = own(n - r) + down.astype(F32)
    total = own(0) + up.astype(F32) + down.astype(F32)
    mine = lax.dynamic_index_in_dim(total, yl, 0, keepdims=False)
    other = lax.dynamic_index_in_dim(total, 1 - yl, 0, keepdims=False)
    both = mine + moved(other.astype(BF16), "yl", 1).astype(F32)
    rows = part_of(both, c, rows_here, 0)
    pair = moved(part_of(both, 1 - c, rows_here, 0), "c", 1)
    return joined(rows, pair, c, 1)


def per_device(
    query_states,
    key_states,
    value_states,
    residual,
    norm_gains,
    lang_labels,
    doc_lengths,
    destinations,
    gate_weight,
    up_weight,
    down_weight,
    out_cotangent,
):
    groups = lax.axis_size(DP)
    my_group = lax.axis_index(DP)
    c, yl = lax.axis_index("c"), lax.axis_index("yl")
    total_units = destinations.shape[0]
    per_group = total_units // groups
    columns = query_states.shape[1]
    width = gate_weight.shape[0]
    tok_group = per_group * UNIT
    rows_here = out_cotangent.shape[0]
    half = width // 2
    gate_t = gate_weight.T
    up_t = up_weight.T

    pair_rows = moved(part_of(out_cotangent, 1 - c, half, 1), "c", 1)
    chip_rows = joined(part_of(out_cotangent, c, half, 1), pair_rows, c, 0)
    run_rows = gathered_over_z(chip_rows).reshape(-1, half)
    cot_half = joined(run_rows, moved(run_rows, "yl", 1), yl, 0)
    cot_full = joined(cot_half, moved(cot_half, "c", 1), c, 1)

    doc_ids = doc_index(doc_lengths, UNIT)
    unit_index = jnp.arange(total_units, dtype=jnp.int32)
    source_group = unit_index // per_group
    earlier = unit_index[None, :] < unit_index[:, None]
    same_target = destinations[None, :] == destinations[:, None]
    same_source = source_group[None, :] == source_group[:, None]
    send_rank = jnp.sum((earlier & same_target & same_source).astype(jnp.int32), axis=1)
    arrival = jnp.sum((earlier & same_target).astype(jnp.int32), axis=1)
    first_unit = my_group * per_group
    own_targets = lax.dynamic_slice_in_dim(destinations, first_unit, per_group)
    own_ranks = lax.dynamic_slice_in_dim(send_rank, first_unit, per_group)
    group_ids = jnp.arange(groups, dtype=jnp.int32)
    slot_ids = jnp.arange(CAP, dtype=jnp.int32)
    send_table = (
        (own_targets[None, None, :] == group_ids[:, None, None])
        & (own_ranks[None, None, :] == slot_ids[None, :, None])
    ).astype(BF16)
    arrive_ids = jnp.arange(per_group, dtype=jnp.int32)
    landing = (destinations == my_group)[None, :] & (arrival[None, :] == arrive_ids[:, None])
    recv_table = jnp.sum(
        (
            landing[:, None, None, :]
            & (source_group[None, None, None, :] == group_ids[None, :, None, None])
            & (send_rank[None, None, None, :] == slot_ids[None, None, :, None])
        ).astype(jnp.int32),
        axis=3,
    ).astype(BF16)
    moved_langs = jnp.sum(landing.astype(jnp.int32) * lang_labels[None, :], axis=1)
    unit_shape = (per_group, UNIT, columns)
    own_docs = lax.dynamic_slice_in_dim(doc_ids, first_unit, per_group, 0)
    local_mix = attend(
        query_states.reshape(unit_shape),
        key_states.reshape(unit_shape),
        value_states.reshape(unit_shape),
        residual.reshape(unit_shape),
        own_docs,
    )
    packed = jnp.einsum(
        "tsu,uic->tsic", send_table, local_mix, preferred_element_type=F32
    ).astype(BF16)
    arrived = lax.all_to_all(packed, DP, split_axis=0, concat_axis=0, tiled=True)
    stream_cols = (
        jnp.einsum("jts,tsic->jic", recv_table, arrived, preferred_element_type=F32)
        .astype(BF16)
        .reshape(tok_group, columns)
    )

    run_cols = gathered_over_z(stream_cols)
    both_yl = joined(run_cols[None], moved(run_cols, "yl", 1)[None], yl, 0)
    both_c = joined(both_yl[:, :, None], moved(both_yl, "c", 1)[:, :, None], c, 2)
    stream = both_c.transpose(3, 0, 1, 2, 4).reshape(tok_group, width)

    langs = jnp.arange(norm_gains.shape[0], dtype=jnp.int32)
    unit_gain = jnp.sum(
        jnp.where((moved_langs[:, None] == langs[None, :])[:, :, None], norm_gains[None], 0.0),
        axis=1,
    )
    gain_tokens = jnp.broadcast_to(unit_gain[:, None], (per_group, UNIT, width)).reshape(
        tok_group, width
    )
    stream_f = stream.astype(F32)
    scaled = (stream_f * gain_tokens).astype(BF16)
    inv_rms = lax.rsqrt(jnp.sum(stream_f * stream_f, axis=1) / width + 1e-05)

    nt = (((1,), (1,)), ((), ()))
    tn = (((0,), (0,)), ((), ()))
    grad_hidden = lax.dot_general(down_weight, cot_full, nt, preferred_element_type=F32)
    gate_acc = lax.dot_general(gate_t, scaled, nt, preferred_element_type=F32)
    up_acc = lax.dot_general(up_t, scaled, nt, preferred_element_type=F32)
    rms_row = inv_rms[None, :]
    act_gate = rms_row * gate_acc
    act_up = rms_row * up_acc
    sigma = jax.nn.sigmoid(act_gate)
    silu = act_gate * sigma
    hidden = (silu * act_up).astype(BF16)
    scaled_grad = rms_row * grad_hidden
    grad_gate = (scaled_grad * act_up * sigma * (1.0 + act_gate * (1.0 - sigma))).astype(BF16)
    grad_up = (scaled_grad * silu).astype(BF16)

    cot_blocks = column_blocks(cot_full, width // groups)
    scaled_blocks = column_blocks(scaled, width // groups)
    hidden_all = gathered_over_x(hidden)
    gate_all = gathered_over_x(grad_gate)
    up_all = gathered_over_x(grad_up)

    out_part = lax.dot_general(hidden, down_weight, tn, preferred_element_type=F32).astype(BF16)
    back_part = (
        lax.dot_general(grad_gate, gate_t, tn, preferred_element_type=F32)
        + lax.dot_general(grad_up, up_t, tn, preferred_element_type=F32)
    ).astype(BF16)
    out_total = row_sums(out_part, rows_here)
    back_total = row_sums(back_part, rows_here)

    down_grad = weight_grad(hidden_all, cot_blocks)
    gate_grad = weight_grad(gate_all, scaled_blocks).T
    up_grad = weight_grad(up_all, scaled_blocks).T

    my_start = lax.axis_index(TENSOR) * rows_here
    rows = lambda a: lax.dynamic_slice_in_dim(a, my_start, rows_here, 0)
    stream_rows = rows(stream).astype(F32)
    scaled_rows = rows(scaled).astype(F32)
    gain_rows = rows(gain_tokens)
    rms_rows = rows(inv_rms)
    layer_out = (stream_rows + out_total).astype(BF16)
    dot_sum = jnp.sum(scaled_rows * back_total, axis=1)
    input_grad = (
        out_cotangent.astype(F32)
        + gain_rows * back_total
        - (rms_rows * rms_rows / width)[:, None] * stream_rows * dot_sum[:, None]
    ).astype(BF16)
    return (layer_out, input_grad, gate_grad, up_grad, down_grad)


def solution(mesh):
    finer = Mesh(mesh.devices.reshape(mesh.shape["dp"] // 2, 2, 2, -1, 2), DP_TENSOR)
    head_cols = P(DP, TENSOR)
    return jax.shard_map(
        per_device,
        mesh=finer,
        in_specs=(
            head_cols,
            head_cols,
            head_cols,
            head_cols,
            P(),
            P(),
            P(),
            P(),
            P(None, TENSOR),
            P(None, TENSOR),
            P(TENSOR, None),
            P(DP_TENSOR, None),
        ),
        out_specs=(
            P(DP_TENSOR, None),
            P(DP_TENSOR, None),
            P(DP, TENSOR),
            P(DP, TENSOR),
            P(TENSOR, DP),
        ),
        check_vma=False,
    )
```

```python
import math

import jax
import jax.numpy as jnp
from jax import lax
from jax.experimental import pallas as pl
from jax.experimental.pallas import tpu as pltpu
from jax.sharding import Mesh
from jax.sharding import PartitionSpec as P

UNIT = 48
CAP = 2
WIN = 24
DP = ("x", "yh")
TENSOR = ("yl", "z", "c")
DP_TENSOR = ("x", "yh", "yl", "z", "c")
F32 = jnp.float32
BF16 = jnp.bfloat16


def moved(array, axis, step):
    n = lax.axis_size(axis)
    return lax.ppermute(array, axis, [(i, (i + step) % n) for i in range(n)])


def joined(mine, other, index, dim):
    return jnp.where(
        index == 0,
        jnp.concatenate([mine, other], axis=dim),
        jnp.concatenate([other, mine], axis=dim),
    )


def sent_over_z(piece):
    n = lax.axis_size("z")
    return lax.all_to_all(jnp.broadcast_to(piece[None], (n, *piece.shape)), "z", 0, 0, tiled=True)


def ring_over_z(piece):
    n = lax.axis_size("z")
    pieces = [piece] * n
    above = below = piece
    for r in range(1, n // 2):
        above = moved(above, "z", -1)
        below = moved(below, "z", 1)
        pieces[r] = above
        pieces[n - r] = below
    far = moved(above[:1], "z", -1), moved(below[1:], "z", 1)
    pieces[n // 2] = jnp.concatenate(far, axis=0)
    return jnp.stack(pieces)


def assembled(mine, other, unit_gain):
    n, halves, tokens, lanes = mine.shape
    units = unit_gain.shape[0]
    per_unit = tokens // units
    width = halves * n * 2 * lanes

    def kernel(at_ref, mine_ref, other_ref, gain_ref, stream_ref, scaled_ref, square_ref):
        step = pl.program_id(0)

        def write(first, second):
            for k, block in enumerate((first, second)):
                cols = slice(k * lanes, (k + 1) * lanes)
                stream_ref[:, cols] = block
                wide = block.astype(F32)
                squares = wide * wide
                if k == 0:
                    total = squares
                else:
                    total = total + squares
                for u in range(units):
                    rows = slice(u * per_unit, (u + 1) * per_unit)
                    scaled_ref[rows, cols] = (wide[rows] * gain_ref[u : u + 1, cols]).astype(BF16)

            @pl.when(step == 0)
            def _():
                square_ref[...] = total

            @pl.when(step > 0)
            def _():
                square_ref[...] += total

        @pl.when(at_ref[1] == 0)
        def _():
            write(mine_ref[0, 0], other_ref[0, 0])

        @pl.when(at_ref[1] == 1)
        def _():
            write(other_ref[0, 0], mine_ref[0, 0])

    def piece(i, at):
        return (lax.rem(lax.rem(i, n) - at[0] + n, n), i // n, 0, 0)

    at = jnp.stack([lax.axis_index("z"), lax.axis_index("c")]).astype(jnp.int32)
    block = pl.BlockSpec((tokens, 2 * lanes), lambda i, at: (0, i))
    return pl.pallas_call(
        kernel,
        grid_spec=pltpu.PrefetchScalarGridSpec(
            num_scalar_prefetch=1,
            grid=(halves * n,),
            in_specs=[
                pl.BlockSpec((1, 1, tokens, lanes), piece),
                pl.BlockSpec((1, 1, tokens, lanes), piece),
                pl.BlockSpec((units, 2 * lanes), lambda i, at: (0, i)),
            ],
            out_specs=[block, block, pl.BlockSpec((tokens, lanes), lambda i, at: (0, 0))],
        ),
        out_shape=[
            jax.ShapeDtypeStruct((tokens, width), BF16),
            jax.ShapeDtypeStruct((tokens, width), BF16),
            jax.ShapeDtypeStruct((tokens, lanes), F32),
        ],
        name="assembled",
    )(at, mine, other, unit_gain)


def finished(sums, pair_sums, stream, unit_gain, out_cotangent):
    rows, width = out_cotangent.shape
    half = width // 2
    per_unit = stream.shape[0] // unit_gain.shape[0]

    def kernel(at_ref, sums_ref, pair_ref, stream_ref, gain_ref, cot_ref, out_ref, grad_ref):
        core = at_ref[1]
        gain = gain_ref[pl.ds(at_ref[2], 1), :]

        def work(first_ref, second_ref, row_at):
            kept = stream_ref[...].astype(F32)[row_at : row_at + rows]
            inv = lax.rsqrt(jnp.sum(kept * kept, axis=1, keepdims=True) / width + 1e-05)
            dots = jnp.zeros((rows, 1), F32)
            for k, ref in enumerate((first_ref, second_ref)):
                cols = slice(k * half, (k + 1) * half)
                scaled = (kept[:, cols] * gain[:, cols]).astype(BF16).astype(F32)
                dots += jnp.sum(scaled * ref[1], axis=1, keepdims=True)
            factor = inv * inv / width * dots
            for k, ref in enumerate((first_ref, second_ref)):
                cols = slice(k * half, (k + 1) * half)
                out_ref[:, cols] = (kept[:, cols] + ref[0]).astype(BF16)
                grad_ref[:, cols] = (
                    cot_ref[:, cols].astype(F32)
                    + gain[:, cols] * ref[1]
                    - factor * kept[:, cols]
                ).astype(BF16)

        @pl.when(core == 0)
        def _():
            work(sums_ref, pair_ref, 0)

        @pl.when(core == 1)
        def _():
            work(pair_ref, sums_ref, rows)

    tensor = lax.axis_index(TENSOR)
    at = jnp.stack([tensor // 2, lax.axis_index("c"), tensor * rows // per_unit]).astype(jnp.int32)
    whole = pl.BlockSpec((2, rows, half), lambda i, at: (0, 0, 0))
    out = pl.BlockSpec((rows, width), lambda i, at: (0, 0))
    return pl.pallas_call(
        kernel,
        grid_spec=pltpu.PrefetchScalarGridSpec(
            num_scalar_prefetch=1,
            grid=(1,),
            in_specs=[
                whole,
                whole,
                pl.BlockSpec((2 * rows, width), lambda i, at: (at[0], 0)),
                pl.BlockSpec(unit_gain.shape, lambda i, at: (0, 0)),
                out,
            ],
            out_specs=[out, out],
        ),
        out_shape=[jax.ShapeDtypeStruct((rows, width), BF16)] * 2,
        name="finished",
    )(at, sums, pair_sums, stream, unit_gain, out_cotangent)


def part_of(array, index, size, dim):
    return lax.dynamic_slice_in_dim(array, index * size, size, dim)


def doc_index(doc_lengths, unit_len):
    doc_ends = jnp.cumsum(doc_lengths, axis=1)
    positions = jnp.arange(unit_len, dtype=jnp.int32)
    return jnp.sum((doc_ends[:, None, :] <= positions[None, :, None]).astype(jnp.int32), axis=2)


def attend(query_units, key_units, value_units, resid_units, doc_units):
    head = query_units.shape[2]
    scores = jnp.einsum(
        "uqd,ukd->uqk", query_units, key_units, preferred_element_type=F32
    ) / math.sqrt(head)
    positions = jnp.arange(query_units.shape[1], dtype=jnp.int32)
    distance = positions[:, None] - positions[None, :]
    allowed = (doc_units[:, :, None] == doc_units[:, None, :]) & (
        (distance >= 0) & (distance < WIN)
    )[None]
    scores = jnp.where(allowed, scores, -1e30)
    row_max = jnp.max(scores, axis=2, keepdims=True)
    exp_scores = jnp.exp(scores - row_max)
    attn_probs = (exp_scores / jnp.sum(exp_scores, axis=2, keepdims=True)).astype(BF16)
    mixed = jnp.einsum("uqk,ukd->uqd", attn_probs, value_units, preferred_element_type=F32)
    return (resid_units.astype(F32) + mixed).astype(BF16)


def column_blocks(full, width):
    x, c = lax.axis_index("x"), lax.axis_index("c")
    n = lax.axis_size("x")

    def block(s, core):
        return part_of(full, 2 * ((x + s) % n) + core, width, 1)

    below = moved(block(1, c), "x", 1)
    above = moved(block(n - 1, c), "x", -1)
    across = moved(block(2, c), "x", 2)
    got = jnp.stack([above, below, across])
    other = moved(got, "c", 1)
    mine = jnp.concatenate([block(0, c), above, below, across], axis=0)
    theirs = jnp.concatenate([block(0, 1 - c), other[0], other[1], other[2]], axis=0)
    same = c == lax.axis_index("yh")
    return jnp.where(same, mine, theirs), jnp.where(same, theirs, mine)


def gathered_over_x(factor):
    half = factor.shape[0] // 2
    below = moved(factor, "x", 1)
    above = moved(factor, "x", -1)
    upper = moved(below[:half], "x", 1)
    lower = moved(above[half:], "x", -1)
    across = jnp.concatenate([upper, lower], axis=0)
    return jnp.concatenate([factor, above, below, across], axis=1)


def weight_grad(factor_all, blocks):
    keep, send = blocks
    sent = jnp.dot(factor_all, send, preferred_element_type=F32).astype(BF16)
    arrived = moved(sent, "yh", 1)
    kept = jnp.dot(factor_all, keep, preferred_element_type=F32)
    return (kept + arrived.astype(F32)).astype(BF16)


def row_sums(parts, rows_here):
    c, z, yl = lax.axis_index("c"), lax.axis_index("z"), lax.axis_index("yl")
    n = lax.axis_size("z")
    half = parts[0].shape[1] // 2
    chip = 2 * rows_here
    shape = (2, n, chip, half)
    pairs = []
    for part in parts:
        arrived = moved(part_of(part, 1 - c, half, 1), "c", 1)
        pairs += [(part_of(part, c, half, 1).reshape(shape), arrived.reshape(shape))]

    def own(r):
        at = (z + r) % n
        pick = lambda a: lax.dynamic_slice_in_dim(a, at, 1, 1)[:, 0].astype(F32)
        return jnp.stack([pick(kept) + pick(arrived) for kept, arrived in pairs], axis=1)

    far = own(n // 2).astype(BF16)
    up = moved(far[0], "z", 1)
    down = moved(far[1], "z", -1)
    near = own(n // 2 - 1)
    up = jnp.stack([near[0] + up.astype(F32), near[1]])
    near = own(n - n // 2 + 1)
    down = jnp.stack([near[0], near[1] + down.astype(F32)])
    for r in range(n // 2 - 2, -1, -1):
        up = moved(up.astype(BF16), "z", 1)
        down = moved(down.astype(BF16), "z", -1)
        if r:
            up = own(r) + up.astype(F32)
            down = own(n - r) + down.astype(F32)
    total = own(0) + up.astype(F32) + down.astype(F32)
    mine = lax.dynamic_index_in_dim(total, yl, 0, keepdims=False)
    other = lax.dynamic_index_in_dim(total, 1 - yl, 0, keepdims=False)
    both = mine + moved(other.astype(BF16), "yl", 1).astype(F32)
    rows = part_of(both, c, rows_here, 1)
    return rows, moved(part_of(both, 1 - c, rows_here, 1), "c", 1)


def per_device(
    query_states,
    key_states,
    value_states,
    residual,
    norm_gains,
    lang_labels,
    doc_lengths,
    destinations,
    gate_weight,
    up_weight,
    down_weight,
    out_cotangent,
):
    groups = lax.axis_size(DP)
    my_group = lax.axis_index(DP)
    c, yl = lax.axis_index("c"), lax.axis_index("yl")
    total_units = destinations.shape[0]
    per_group = total_units // groups
    columns = query_states.shape[1]
    width = gate_weight.shape[0]
    tok_group = per_group * UNIT
    rows_here = out_cotangent.shape[0]
    half = width // 2
    gate_t = gate_weight.T
    up_t = up_weight.T

    pair_rows = moved(part_of(out_cotangent, 1 - c, half, 1), "c", 1)
    chip_rows = joined(part_of(out_cotangent, c, half, 1), pair_rows, c, 0)
    run_rows = sent_over_z(chip_rows).reshape(-1, half)
    cot_half = joined(run_rows, moved(run_rows, "yl", 1), yl, 0)
    cot_full = joined(cot_half, moved(cot_half, "c", 1), c, 1)

    doc_ids = doc_index(doc_lengths, UNIT)
    unit_index = jnp.arange(total_units, dtype=jnp.int32)
    source_group = unit_index // per_group
    earlier = unit_index[None, :] < unit_index[:, None]
    same_target = destinations[None, :] == destinations[:, None]
    same_source = source_group[None, :] == source_group[:, None]
    send_rank = jnp.sum((earlier & same_target & same_source).astype(jnp.int32), axis=1)
    arrival = jnp.sum((earlier & same_target).astype(jnp.int32), axis=1)
    first_unit = my_group * per_group
    own_targets = lax.dynamic_slice_in_dim(destinations, first_unit, per_group)
    own_ranks = lax.dynamic_slice_in_dim(send_rank, first_unit, per_group)
    group_ids = jnp.arange(groups, dtype=jnp.int32)
    slot_ids = jnp.arange(CAP, dtype=jnp.int32)
    send_table = (
        (own_targets[None, None, :] == group_ids[:, None, None])
        & (own_ranks[None, None, :] == slot_ids[None, :, None])
    ).astype(BF16)
    arrive_ids = jnp.arange(per_group, dtype=jnp.int32)
    landing = (destinations == my_group)[None, :] & (arrival[None, :] == arrive_ids[:, None])
    recv_table = jnp.sum(
        (
            landing[:, None, None, :]
            & (source_group[None, None, None, :] == group_ids[None, :, None, None])
            & (send_rank[None, None, None, :] == slot_ids[None, None, :, None])
        ).astype(jnp.int32),
        axis=3,
    ).astype(BF16)
    moved_langs = jnp.sum(landing.astype(jnp.int32) * lang_labels[None, :], axis=1)
    unit_shape = (per_group, UNIT, columns)
    own_docs = lax.dynamic_slice_in_dim(doc_ids, first_unit, per_group, 0)
    local_mix = attend(
        query_states.reshape(unit_shape),
        key_states.reshape(unit_shape),
        value_states.reshape(unit_shape),
        residual.reshape(unit_shape),
        own_docs,
    )
    packed = jnp.einsum(
        "tsu,uic->tsic", send_table, local_mix, preferred_element_type=F32
    ).astype(BF16)
    arrived = lax.all_to_all(packed, DP, split_axis=0, concat_axis=0, tiled=True)
    stream_cols = (
        jnp.einsum("jts,tsic->jic", recv_table, arrived, preferred_element_type=F32)
        .astype(BF16)
        .reshape(tok_group, columns)
    )

    langs = jnp.arange(norm_gains.shape[0], dtype=jnp.int32)
    unit_gain = jnp.sum(
        jnp.where((moved_langs[:, None] == langs[None, :])[:, :, None], norm_gains[None], 0.0),
        axis=1,
    )
    both_yl = joined(stream_cols[None], moved(stream_cols, "yl", 1)[None], yl, 0)
    run_cols = ring_over_z(both_yl)
    stream, scaled, squares = assembled(run_cols, moved(run_cols, "c", 1), unit_gain)
    inv_rms = lax.rsqrt(jnp.sum(squares, axis=1) / width + 1e-05)

    nt = (((1,), (1,)), ((), ()))
    tn = (((0,), (0,)), ((), ()))
    grad_hidden = lax.dot_general(down_weight, cot_full, nt, preferred_element_type=F32)
    gate_acc = lax.dot_general(gate_t, scaled, nt, preferred_element_type=F32)
    up_acc = lax.dot_general(up_t, scaled, nt, preferred_element_type=F32)
    rms_row = inv_rms[None, :]
    act_gate = rms_row * gate_acc
    act_up = rms_row * up_acc
    sigma = jax.nn.sigmoid(act_gate)
    silu = act_gate * sigma
    hidden = (silu * act_up).astype(BF16)
    scaled_grad = rms_row * grad_hidden
    grad_gate = (scaled_grad * act_up * sigma * (1.0 + act_gate * (1.0 - sigma))).astype(BF16)
    grad_up = (scaled_grad * silu).astype(BF16)

    cot_blocks = column_blocks(cot_full, width // groups)
    scaled_blocks = column_blocks(scaled, width // groups)
    hidden_all = gathered_over_x(hidden)
    gate_up_all = gathered_over_x(jnp.concatenate([grad_gate, grad_up], axis=0))

    out_part = lax.dot_general(hidden, down_weight, tn, preferred_element_type=F32).astype(BF16)
    back_part = (
        lax.dot_general(grad_gate, gate_t, tn, preferred_element_type=F32)
        + lax.dot_general(grad_up, up_t, tn, preferred_element_type=F32)
    ).astype(BF16)
    sums, pair_sums = row_sums([out_part, back_part], rows_here)

    down_grad = weight_grad(hidden_all, cot_blocks)
    gate_up_grad = weight_grad(gate_up_all, scaled_blocks)
    hidden_here = gate_weight.shape[1]
    gate_grad = gate_up_grad[:hidden_here].T
    up_grad = gate_up_grad[hidden_here:].T
    layer_out, input_grad = finished(sums, pair_sums, stream, unit_gain, out_cotangent)
    return (layer_out, input_grad, gate_grad, up_grad, down_grad)


def solution(mesh):
    finer = Mesh(mesh.devices.reshape(mesh.shape["dp"] // 2, 2, 2, -1, 2), DP_TENSOR)
    head_cols = P(DP, TENSOR)
    return jax.shard_map(
        per_device,
        mesh=finer,
        in_specs=(
            head_cols,
            head_cols,
            head_cols,
            head_cols,
            P(),
            P(),
            P(),
            P(),
            P(None, TENSOR),
            P(None, TENSOR),
            P(TENSOR, None),
            P(DP_TENSOR, None),
        ),
        out_specs=(
            P(DP_TENSOR, None),
            P(DP_TENSOR, None),
            P(DP, TENSOR),
            P(DP, TENSOR),
            P(TENSOR, DP),
        ),
        check_vma=False,
    )
```

```python
import math

import jax
import jax.numpy as jnp
from jax import lax
from jax.experimental import pallas as pl
from jax.experimental.pallas import tpu as pltpu
from jax.sharding import Mesh
from jax.sharding import PartitionSpec as P

UNIT = 48
WIN = 24
DP = ("x", "yh")
TENSOR = ("yl", "z", "c")
DP_TENSOR = ("x", "yh", "yl", "z", "c")
F32 = jnp.float32
BF16 = jnp.bfloat16


def moved(array, axis, step):
    n = lax.axis_size(axis)
    return lax.ppermute(array, axis, [(i, (i + step) % n) for i in range(n)])


def joined(mine, other, index, dim):
    return jnp.where(
        index == 0,
        jnp.concatenate([mine, other], axis=dim),
        jnp.concatenate([other, mine], axis=dim),
    )


def sent_over_z(piece):
    n = lax.axis_size("z")
    return lax.all_to_all(jnp.broadcast_to(piece[None], (n, *piece.shape)), "z", 0, 0, tiled=True)


def ring_over_z(piece, beside):
    n = lax.axis_size("z")
    pieces = [piece] * n
    above = below = piece
    for r in range(1, n // 2):
        if r == n // 2 - 1:
            (above, below), beside = lax.optimization_barrier(((above, below), beside))
        above = moved(above, "z", -1)
        below = moved(below, "z", 1)
        pieces[r] = above
        pieces[n - r] = below
    far = moved(above[:1], "z", -1), moved(below[1:], "z", 1)
    pieces[n // 2] = jnp.concatenate(far, axis=0)
    return jnp.stack(pieces), beside


def assembled(mine, other, unit_gain):
    n, halves, tokens, lanes = mine.shape
    units = unit_gain.shape[0]
    per_unit = tokens // units
    width = 2 * n * halves * lanes
    run = n // 2

    def kernel(at_ref, *refs):
        mine_refs, other_refs = refs[:run], refs[run : 2 * run]
        gain_ref, stream_ref, scaled_ref, square_ref = refs[2 * run :]

        def write(first_refs, second_refs):
            total = jnp.zeros((tokens, lanes), F32)
            for k in range(2 * run):
                block = (first_refs, second_refs)[k % 2][k // 2][0, 0]
                cols = slice(k * lanes, (k + 1) * lanes)
                stream_ref[:, cols] = block
                wide = block.astype(F32)
                total += wide * wide
                for u in range(units):
                    rows = slice(u * per_unit, (u + 1) * per_unit)
                    scaled_ref[rows, cols] = (wide[rows] * gain_ref[u : u + 1, cols]).astype(BF16)

            @pl.when(pl.program_id(0) == 0)
            def _():
                square_ref[...] = total

            @pl.when(pl.program_id(0) > 0)
            def _():
                square_ref[...] += total

        @pl.when(at_ref[1] == 0)
        def _():
            write(mine_refs, other_refs)

        @pl.when(at_ref[1] == 1)
        def _():
            write(other_refs, mine_refs)

    def piece(k):
        return pl.BlockSpec(
            (1, 1, tokens, lanes),
            lambda i, at: (lax.rem((i % 2) * run + k - at[0] + n, n), i // 2, 0, 0),
        )

    at = jnp.stack([lax.axis_index("z"), lax.axis_index("c")]).astype(jnp.int32)
    wide_block = run * 2 * lanes
    block = pl.BlockSpec((tokens, wide_block), lambda i, at: (0, i))
    return pl.pallas_call(
        kernel,
        grid_spec=pltpu.PrefetchScalarGridSpec(
            num_scalar_prefetch=1,
            grid=(halves * 2,),
            in_specs=[piece(k) for k in range(run)] * 2
            + [pl.BlockSpec((units, wide_block), lambda i, at: (0, i))],
            out_specs=[block, block, pl.BlockSpec((tokens, lanes), lambda i, at: (0, 0))],
        ),
        out_shape=[
            jax.ShapeDtypeStruct((tokens, width), BF16),
            jax.ShapeDtypeStruct((tokens, width), BF16),
            jax.ShapeDtypeStruct((tokens, lanes), F32),
        ],
        name="assembled",
    )(at, *[mine] * run, *[other] * run, unit_gain)


def finished(sums, pair_sums, stream, unit_gain, out_cotangent):
    rows, width = out_cotangent.shape
    half = width // 2
    per_unit = stream.shape[0] // unit_gain.shape[0]

    def kernel(at_ref, sums_ref, pair_ref, stream_ref, gain_ref, cot_ref, out_ref, grad_ref):
        core = at_ref[1]
        gain = gain_ref[pl.ds(at_ref[2], 1), :]

        def work(first_ref, second_ref, row_at):
            kept = stream_ref[...].astype(F32)[row_at : row_at + rows]
            inv = lax.rsqrt(jnp.sum(kept * kept, axis=1, keepdims=True) / width + 1e-05)
            dots = jnp.zeros((rows, 1), F32)
            for k, ref in enumerate((first_ref, second_ref)):
                cols = slice(k * half, (k + 1) * half)
                scaled = (kept[:, cols] * gain[:, cols]).astype(BF16).astype(F32)
                dots += jnp.sum(scaled * ref[1], axis=1, keepdims=True)
            factor = inv * inv / width * dots
            for k, ref in enumerate((first_ref, second_ref)):
                cols = slice(k * half, (k + 1) * half)
                out_ref[:, cols] = (kept[:, cols] + ref[0]).astype(BF16)
                grad_ref[:, cols] = (
                    cot_ref[:, cols].astype(F32)
                    + gain[:, cols] * ref[1]
                    - factor * kept[:, cols]
                ).astype(BF16)

        @pl.when(core == 0)
        def _():
            work(sums_ref, pair_ref, 0)

        @pl.when(core == 1)
        def _():
            work(pair_ref, sums_ref, rows)

    tensor = lax.axis_index(TENSOR)
    at = jnp.stack([tensor // 2, lax.axis_index("c"), tensor * rows // per_unit]).astype(jnp.int32)
    whole = pl.BlockSpec((2, rows, half), lambda i, at: (0, 0, 0))
    out = pl.BlockSpec((rows, width), lambda i, at: (0, 0))
    return pl.pallas_call(
        kernel,
        grid_spec=pltpu.PrefetchScalarGridSpec(
            num_scalar_prefetch=1,
            grid=(1,),
            in_specs=[
                whole,
                whole,
                pl.BlockSpec((2 * rows, width), lambda i, at: (at[0], 0)),
                pl.BlockSpec(unit_gain.shape, lambda i, at: (0, 0)),
                out,
            ],
            out_specs=[out, out],
        ),
        out_shape=[jax.ShapeDtypeStruct((rows, width), BF16)] * 2,
        name="finished",
    )(at, sums, pair_sums, stream, unit_gain, out_cotangent)


def part_of(array, index, size, dim):
    return lax.dynamic_slice_in_dim(array, index * size, size, dim)


def doc_index(doc_lengths, unit_len):
    doc_ends = jnp.cumsum(doc_lengths, axis=1)
    positions = jnp.arange(unit_len, dtype=jnp.int32)
    return jnp.sum((doc_ends[:, None, :] <= positions[None, :, None]).astype(jnp.int32), axis=2)


def attend(query_units, key_units, value_units, resid_units, doc_units):
    head = query_units.shape[2]
    scores = jnp.einsum(
        "uqd,ukd->uqk", query_units, key_units, preferred_element_type=F32
    ) / math.sqrt(head)
    positions = jnp.arange(query_units.shape[1], dtype=jnp.int32)
    distance = positions[:, None] - positions[None, :]
    allowed = (doc_units[:, :, None] == doc_units[:, None, :]) & (
        (distance >= 0) & (distance < WIN)
    )[None]
    scores = jnp.where(allowed, scores, -1e30)
    row_max = jnp.max(scores, axis=2, keepdims=True)
    exp_scores = jnp.exp(scores - row_max)
    attn_probs = (exp_scores / jnp.sum(exp_scores, axis=2, keepdims=True)).astype(BF16)
    mixed = jnp.einsum("uqk,ukd->uqd", attn_probs, value_units, preferred_element_type=F32)
    return (resid_units.astype(F32) + mixed).astype(BF16)


def columns_over_x(full, width):
    x, c = lax.axis_index("x"), lax.axis_index("c")
    n = lax.axis_size("x")

    def block(s, core):
        return part_of(full, 2 * ((x + s) % n) + core, width, 1)

    below = moved(block(1, c), "x", 1)
    above = moved(block(n - 1, c), "x", -1)
    across = moved(block(2, c), "x", 2)
    return (block(0, c), block(0, 1 - c)), (above, below, across)


def column_blocks(blocks, arrived, sent):
    own, pair_own = blocks
    got = jnp.stack(held_until(arrived, *sent))
    other = moved(got, "c", 1)
    mine = jnp.concatenate([own, got[0], got[1], got[2]], axis=0)
    theirs = jnp.concatenate([pair_own, other[0], other[1], other[2]], axis=0)
    same = lax.axis_index("c") == lax.axis_index("yh")
    return jnp.where(same, mine, theirs), jnp.where(same, theirs, mine)


def held_until(values, *others):
    return lax.optimization_barrier((values, *others))[0]


def gathered_over_x(factor, near, sent, sent_later):
    half = factor.shape[0] // 2
    below, above = held_until(near, *sent)
    upper = moved(below[:half], "x", 1)
    lower = moved(above[half:], "x", -1)
    upper, lower = held_until((upper, lower), *sent_later)
    across = jnp.concatenate([upper, lower], axis=0)
    return jnp.concatenate([factor, above, below, across], axis=1)


def near_over_x(factor):
    return moved(factor, "x", 1), moved(factor, "x", -1)


def weight_grad(factor_all, blocks):
    keep, send = blocks
    part = jnp.dot(factor_all, send, preferred_element_type=F32).astype(BF16)
    arrived = moved(part, "yh", 1)
    kept = jnp.dot(factor_all, keep, preferred_element_type=F32)
    return (kept + arrived.astype(F32)).astype(BF16)


def row_sums(parts, rows_here):
    c, z, yl = lax.axis_index("c"), lax.axis_index("z"), lax.axis_index("yl")
    n = lax.axis_size("z")
    half = parts[0].shape[1] // 2
    chip = 2 * rows_here
    shape = (2, n, chip, half)
    pairs = []
    for part in parts:
        arrived = moved(part_of(part, 1 - c, half, 1), "c", 1)
        pairs += [(part_of(part, c, half, 1).reshape(shape), arrived.reshape(shape))]

    def own(r):
        at = (z + r) % n
        pick = lambda a: lax.dynamic_slice_in_dim(a, at, 1, 1)[:, 0].astype(F32)
        return jnp.stack([pick(kept) + pick(arrived) for kept, arrived in pairs], axis=1)

    far = own(n // 2).astype(BF16)
    up = moved(far[0], "z", 1)
    down = moved(far[1], "z", -1)
    near = own(n // 2 - 1)
    up = jnp.stack([near[0] + up.astype(F32), near[1]])
    near = own(n - n // 2 + 1)
    down = jnp.stack([near[0], near[1] + down.astype(F32)])
    sent = []
    for r in range(n // 2 - 2, -1, -1):
        up, down = up.astype(BF16), down.astype(BF16)
        sent += [(up, down)]
        up = moved(up, "z", 1)
        down = moved(down, "z", -1)
        if r:
            up = own(r) + up.astype(F32)
            down = own(n - r) + down.astype(F32)
    total = own(0) + up.astype(F32) + down.astype(F32)
    mine = lax.dynamic_index_in_dim(total, yl, 0, keepdims=False)
    other = lax.dynamic_index_in_dim(total, 1 - yl, 0, keepdims=False)
    both = mine + moved(other.astype(BF16), "yl", 1).astype(F32)
    rows = part_of(both, c, rows_here, 1)
    return rows, moved(part_of(both, 1 - c, rows_here, 1), "c", 1), sent


def per_device(
    query_states,
    key_states,
    value_states,
    residual,
    norm_gains,
    lang_labels,
    doc_lengths,
    destinations,
    gate_weight,
    up_weight,
    down_weight,
    out_cotangent,
):
    groups = lax.axis_size(DP)
    my_group = lax.axis_index(DP)
    c, yl = lax.axis_index("c"), lax.axis_index("yl")
    total_units = destinations.shape[0]
    per_group = total_units // groups
    columns = query_states.shape[1]
    width = gate_weight.shape[0]
    tok_group = per_group * UNIT
    rows_here = out_cotangent.shape[0]
    half = width // 2
    gate_t = gate_weight.T
    up_t = up_weight.T

    pair_rows = moved(part_of(out_cotangent, 1 - c, half, 1), "c", 1)
    chip_rows = joined(part_of(out_cotangent, c, half, 1), pair_rows, c, 0)
    run_rows = sent_over_z(chip_rows).reshape(-1, half)
    doc_ids = doc_index(doc_lengths, UNIT)
    unit_index = jnp.arange(total_units, dtype=jnp.int32)
    earlier = unit_index[None, :] < unit_index[:, None]
    same_target = destinations[None, :] == destinations[:, None]
    arrival = jnp.sum((earlier & same_target).astype(jnp.int32), axis=1)
    first_unit = my_group * per_group
    landing_at = jnp.where(destinations == my_group, arrival, -1)
    arrive_ids = jnp.arange(per_group, dtype=jnp.int32)
    landing = landing_at[None, :] == arrive_ids[:, None]
    moved_langs = jnp.sum(landing.astype(jnp.int32) * lang_labels[None, :], axis=1)
    near_x = (lax.axis_index("x") + jnp.arange(groups // 2, dtype=jnp.int32)) % (groups // 2)
    near_y = (lax.axis_index("yh") + jnp.arange(2, dtype=jnp.int32)) % 2
    held_group = (near_x[:, None] * 2 + near_y[None, :]).reshape(-1)
    held_unit = (held_group[:, None] * per_group + arrive_ids[None, :]).reshape(-1)
    held_at = jnp.sum(
        jnp.where(held_unit[:, None] == unit_index[None, :], landing_at[None, :], 0), axis=1
    )
    pick_table = (held_at[None, :] == arrive_ids[:, None]).astype(BF16)
    unit_shape = (per_group, UNIT, columns)
    own_docs = lax.dynamic_slice_in_dim(doc_ids, first_unit, per_group, 0)
    local_mix = attend(
        query_states.reshape(unit_shape),
        key_states.reshape(unit_shape),
        value_states.reshape(unit_shape),
        residual.reshape(unit_shape),
        own_docs,
    )
    pair_mix = jnp.concatenate([local_mix, moved(local_mix, "yh", 1)], axis=0)
    held = jnp.concatenate(
        [
            pair_mix,
            moved(pair_mix, "x", -1),
            moved(pair_mix, "x", 2),
            moved(pair_mix, "x", 1),
        ],
        axis=0,
    )
    stream_cols = (
        jnp.einsum("ju,uic->jic", pick_table, held, preferred_element_type=F32)
        .astype(BF16)
        .reshape(tok_group, columns)
    )

    langs = jnp.arange(norm_gains.shape[0], dtype=jnp.int32)
    unit_gain = jnp.sum(
        jnp.where((moved_langs[:, None] == langs[None, :])[:, :, None], norm_gains[None], 0.0),
        axis=1,
    )
    both_yl = joined(stream_cols[None], moved(stream_cols, "yl", 1)[None], yl, 0)
    run_cols, run_rows = ring_over_z(both_yl, run_rows)
    cot_half = joined(run_rows, moved(run_rows, "yl", 1), yl, 0)
    cot_full = joined(cot_half, moved(cot_half, "c", 1), c, 1)
    stream, scaled, squares = assembled(run_cols, moved(run_cols, "c", 1), unit_gain)
    nt = (((1,), (1,)), ((), ()))
    tn = (((0,), (0,)), ((), ()))
    grad_hidden = lax.dot_general(down_weight, cot_full, nt, preferred_element_type=F32)
    cot_columns = columns_over_x(cot_full, width // groups)
    scaled_columns = columns_over_x(scaled, width // groups)
    scaled, grad_hidden = lax.optimization_barrier((scaled, grad_hidden))
    inv_rms = lax.rsqrt(jnp.sum(squares, axis=1) / width + 1e-05)
    gate_acc = lax.dot_general(gate_t, scaled, nt, preferred_element_type=F32)
    up_acc = lax.dot_general(up_t, scaled, nt, preferred_element_type=F32)
    rms_row = inv_rms[None, :]
    act_gate = rms_row * gate_acc
    act_up = rms_row * up_acc
    sigma = jax.nn.sigmoid(act_gate)
    silu = act_gate * sigma
    hidden = (silu * act_up).astype(BF16)
    scaled_grad = rms_row * grad_hidden
    grad_gate = (scaled_grad * act_up * sigma * (1.0 + act_gate * (1.0 - sigma))).astype(BF16)
    grad_up = (scaled_grad * silu).astype(BF16)
    gate_up = jnp.concatenate([grad_gate, grad_up], axis=0)

    near_hidden = near_over_x(hidden)
    near_gate_up = near_over_x(gate_up)
    out_part = lax.dot_general(hidden, down_weight, tn, preferred_element_type=F32).astype(BF16)
    back_part = (
        lax.dot_general(grad_gate, gate_t, tn, preferred_element_type=F32)
        + lax.dot_general(grad_up, up_t, tn, preferred_element_type=F32)
    ).astype(BF16)
    sums, pair_sums, sent = row_sums([out_part, back_part], rows_here)

    hidden_all = gathered_over_x(hidden, near_hidden, sent[0], sent[1])
    gate_up_all = gathered_over_x(gate_up, near_gate_up, sent[0], sent[2])
    scaled_blocks = column_blocks(*scaled_columns, sent[0])
    cot_blocks = column_blocks(*cot_columns, sent[0])
    down_grad = weight_grad(hidden_all, cot_blocks)
    gate_up_grad = weight_grad(gate_up_all, scaled_blocks)
    hidden_here = gate_weight.shape[1]
    gate_grad = gate_up_grad[:hidden_here].T
    up_grad = gate_up_grad[hidden_here:].T
    layer_out, input_grad = finished(sums, pair_sums, stream, unit_gain, out_cotangent)
    return (layer_out, input_grad, gate_grad, up_grad, down_grad)


def solution(mesh):
    finer = Mesh(mesh.devices.reshape(mesh.shape["dp"] // 2, 2, 2, -1, 2), DP_TENSOR)
    head_cols = P(DP, TENSOR)
    return jax.shard_map(
        per_device,
        mesh=finer,
        in_specs=(
            head_cols,
            head_cols,
            head_cols,
            head_cols,
            P(),
            P(),
            P(),
            P(),
            P(None, TENSOR),
            P(None, TENSOR),
            P(TENSOR, None),
            P(DP_TENSOR, None),
        ),
        out_specs=(
            P(DP_TENSOR, None),
            P(DP_TENSOR, None),
            P(DP, TENSOR),
            P(DP, TENSOR),
            P(TENSOR, DP),
        ),
        check_vma=False,
    )
```

```python
import math

import jax
import jax.numpy as jnp
from jax import lax
from jax.experimental import pallas as pl
from jax.experimental.pallas import tpu as pltpu
from jax.sharding import Mesh
from jax.sharding import PartitionSpec as P


UNIT = 48
WIN = 24
DP = ("x", "yh")
TENSOR = ("yl", "z", "c")
DP_TENSOR = ("x", "yh", "yl", "z", "c")
F32 = jnp.float32
BF16 = jnp.bfloat16


def moved(array, axis, step):
    n = lax.axis_size(axis)
    return lax.ppermute(array, axis, [(i, (i + step) % n) for i in range(n)])


def joined(mine, other, index, dim):
    return jnp.where(
        index == 0,
        jnp.concatenate([mine, other], axis=dim),
        jnp.concatenate([other, mine], axis=dim),
    )


def sent_over_z(piece):
    n = lax.axis_size("z")
    return lax.all_to_all(jnp.broadcast_to(piece[None], (n, *piece.shape)), "z", 0, 0, tiled=True)


def ring_over_z(piece, rows):
    n = lax.axis_size("z")
    pieces = [piece] * n
    above = below = piece
    for r in range(1, n // 2):
        if r == 2:
            (above, below), rows = lax.optimization_barrier(((above, below), rows))
            pair_rows = moved(rows, "yl", 1)
        above = moved(above, "z", -1)
        below = moved(below, "z", 1)
        pieces[r] = above
        pieces[n - r] = below
    (above, below), pair_rows = lax.optimization_barrier(((above, below), pair_rows))
    far = moved(above[:1], "z", -1), moved(below[1:], "z", 1)
    pieces[n // 2] = jnp.concatenate(far, axis=0)
    return jnp.stack(pieces), rows, pair_rows


def assembled(mine, other, unit_gain):
    n, halves, tokens, lanes = mine.shape
    units = unit_gain.shape[0]
    per_unit = tokens // units
    width = 2 * n * halves * lanes
    run = n // 2

    def kernel(at_ref, *refs):
        mine_refs, other_refs = refs[:run], refs[run : 2 * run]
        gain_ref, stream_ref, scaled_ref, square_ref = refs[2 * run :]

        def write(first_refs, second_refs):
            total = jnp.zeros((tokens, lanes), F32)
            for k in range(2 * run):
                block = (first_refs, second_refs)[k % 2][k // 2][0, 0]
                cols = slice(k * lanes, (k + 1) * lanes)
                stream_ref[:, cols] = block
                wide = block.astype(F32)
                total += wide * wide
                for u in range(units):
                    rows = slice(u * per_unit, (u + 1) * per_unit)
                    scaled_ref[rows, cols] = (wide[rows] * gain_ref[u : u + 1, cols]).astype(BF16)

            @pl.when(pl.program_id(0) == 0)
            def _():
                square_ref[...] = total

            @pl.when(pl.program_id(0) > 0)
            def _():
                square_ref[...] += total

        @pl.when(at_ref[1] == 0)
        def _():
            write(mine_refs, other_refs)

        @pl.when(at_ref[1] == 1)
        def _():
            write(other_refs, mine_refs)

    def piece(k):
        return pl.BlockSpec(
            (1, 1, tokens, lanes),
            lambda i, at: (lax.rem((i % 2) * run + k - at[0] + n, n), i // 2, 0, 0),
        )

    at = jnp.stack([lax.axis_index("z"), lax.axis_index("c")]).astype(jnp.int32)
    wide_block = run * 2 * lanes
    block = pl.BlockSpec((tokens, wide_block), lambda i, at: (0, i))
    return pl.pallas_call(
        kernel,
        grid_spec=pltpu.PrefetchScalarGridSpec(
            num_scalar_prefetch=1,
            grid=(halves * 2,),
            in_specs=[piece(k) for k in range(run)] * 2
            + [pl.BlockSpec((units, wide_block), lambda i, at: (0, i))],
            out_specs=[block, block, pl.BlockSpec((tokens, lanes), lambda i, at: (0, 0))],
        ),
        out_shape=[
            jax.ShapeDtypeStruct((tokens, width), BF16),
            jax.ShapeDtypeStruct((tokens, width), BF16),
            jax.ShapeDtypeStruct((tokens, lanes), F32),
        ],
        compiler_params=pltpu.CompilerParams(vmem_limit_bytes=12 * 2**20),
        name="assembled",
    )(at, *[mine] * run, *[other] * run, unit_gain)


def finished(sums, pair_sums, stream, unit_gain, out_cotangent):
    rows, width = out_cotangent.shape
    half = width // 2
    per_unit = stream.shape[0] // unit_gain.shape[0]

    def kernel(at_ref, sums_ref, pair_ref, stream_ref, gain_ref, cot_ref, out_ref, grad_ref):
        core = at_ref[1]
        gain = gain_ref[pl.ds(at_ref[2], 1), :]

        def work(first_ref, second_ref, row_at):
            kept = stream_ref[...].astype(F32)[row_at : row_at + rows]
            inv = lax.rsqrt(jnp.sum(kept * kept, axis=1, keepdims=True) / width + 1e-05)
            dots = jnp.zeros((rows, 1), F32)
            for k, ref in enumerate((first_ref, second_ref)):
                cols = slice(k * half, (k + 1) * half)
                scaled = (kept[:, cols] * gain[:, cols]).astype(BF16).astype(F32)
                dots += jnp.sum(scaled * ref[1], axis=1, keepdims=True)
            factor = inv * inv / width * dots
            for k, ref in enumerate((first_ref, second_ref)):
                cols = slice(k * half, (k + 1) * half)
                out_ref[:, cols] = (kept[:, cols] + ref[0]).astype(BF16)
                grad_ref[:, cols] = (
                    cot_ref[:, cols].astype(F32)
                    + gain[:, cols] * ref[1]
                    - factor * kept[:, cols]
                ).astype(BF16)

        @pl.when(core == 0)
        def _():
            work(sums_ref, pair_ref, 0)

        @pl.when(core == 1)
        def _():
            work(pair_ref, sums_ref, rows)

    tensor = lax.axis_index(TENSOR)
    at = jnp.stack([tensor // 2, lax.axis_index("c"), tensor * rows // per_unit]).astype(jnp.int32)
    whole = pl.BlockSpec((2, rows, half), lambda i, at: (0, 0, 0))
    out = pl.BlockSpec((rows, width), lambda i, at: (0, 0))
    return pl.pallas_call(
        kernel,
        grid_spec=pltpu.PrefetchScalarGridSpec(
            num_scalar_prefetch=1,
            grid=(1,),
            in_specs=[
                whole,
                whole,
                pl.BlockSpec((2 * rows, width), lambda i, at: (at[0], 0)),
                pl.BlockSpec(unit_gain.shape, lambda i, at: (0, 0)),
                out,
            ],
            out_specs=[out, out],
        ),
        out_shape=[jax.ShapeDtypeStruct((rows, width), BF16)] * 2,
        compiler_params=pltpu.CompilerParams(vmem_limit_bytes=4 * 2**20),
        name="finished",
    )(at, sums, pair_sums, stream, unit_gain, out_cotangent)


def part_of(array, index, size, dim):
    return lax.dynamic_slice_in_dim(array, index * size, size, dim)


def doc_index(doc_lengths, unit_len):
    doc_ends = jnp.cumsum(doc_lengths, axis=1)
    positions = jnp.arange(unit_len, dtype=jnp.int32)
    return jnp.sum((doc_ends[:, None, :] <= positions[None, :, None]).astype(jnp.int32), axis=2)


def attend(query_units, key_units, value_units, resid_units, doc_units):
    head = query_units.shape[2]
    scores = jnp.einsum(
        "uqd,ukd->uqk", query_units, key_units, preferred_element_type=F32
    ) / math.sqrt(head)
    positions = jnp.arange(query_units.shape[1], dtype=jnp.int32)
    distance = positions[:, None] - positions[None, :]
    allowed = (doc_units[:, :, None] == doc_units[:, None, :]) & (
        (distance >= 0) & (distance < WIN)
    )[None]
    scores = jnp.where(allowed, scores, -1e30)
    row_max = jnp.max(scores, axis=2, keepdims=True)
    exp_scores = jnp.exp(scores - row_max)
    attn_probs = (exp_scores / jnp.sum(exp_scores, axis=2, keepdims=True)).astype(BF16)
    mixed = jnp.einsum("uqk,ukd->uqd", attn_probs, value_units, preferred_element_type=F32)
    return (resid_units.astype(F32) + mixed).astype(BF16)


def column_parts(full, width):
    x, c = lax.axis_index("x"), lax.axis_index("c")
    n = lax.axis_size("x")
    block = lambda s, core: part_of(full, 2 * ((x + s) % n) + core, width, 1)
    return (block(0, c), block(0, 1 - c)), (block(1, c), block(n - 1, c), block(2, c))


def columns_over_x(to_send):
    up, down, far = to_send
    return moved(down, "x", -1), moved(up, "x", 1), moved(far, "x", 2)


def column_blocks(own, arrived, other):
    mine = jnp.concatenate([own[0], *arrived], axis=0)
    theirs = jnp.concatenate([own[1], other[0], other[1], other[2]], axis=0)
    same = lax.axis_index("c") == lax.axis_index("yh")
    return jnp.where(same, mine, theirs), jnp.where(same, theirs, mine)


def near_over_x(factor):
    return moved(factor, "x", 1), moved(factor, "x", -1)


def far_over_x(near):
    below, above = near
    half = below.shape[0] // 2
    return moved(below[:half], "x", 1), moved(above[half:], "x", -1)


def all_over_x(factor, near, far):
    below, above = near
    return jnp.concatenate([factor, above, below, jnp.concatenate(far, axis=0)], axis=1)


def pair_share(factor_all, send):
    part = jnp.dot(factor_all, send, preferred_element_type=F32).astype(BF16)
    return moved(part, "yh", 1)


def weight_grad(factor_all, keep, arrived):
    kept = jnp.dot(factor_all, keep, preferred_element_type=F32)
    return (kept + arrived.astype(F32)).astype(BF16)


class RowSums:
    def __init__(self, parts, rows_here):
        self.rows_here = rows_here
        self.c, self.z = lax.axis_index("c"), lax.axis_index("z")
        self.yl = lax.axis_index("yl")
        self.n = lax.axis_size("z")
        half = parts[0].shape[1] // 2
        shape = (2, self.n, 2 * rows_here, half)
        self.pairs = []
        for part in parts:
            arrived = moved(part_of(part, 1 - self.c, half, 1), "c", 1)
            kept = part_of(part, self.c, half, 1)
            self.pairs += [(kept.reshape(shape), arrived.reshape(shape))]

    def own(self, r):
        at = (self.z + r) % self.n
        pick = lambda a: lax.dynamic_slice_in_dim(a, at, 1, 1)[:, 0].astype(F32)
        return jnp.stack([pick(kept) + pick(arrived) for kept, arrived in self.pairs], axis=1)

    def first(self):
        far = self.own(self.n // 2).astype(BF16)
        return far[0], far[1]

    def second(self, up, down):
        near = self.own(self.n // 2 - 1)
        above = jnp.stack([near[0] + up.astype(F32), near[1]])
        near = self.own(self.n - self.n // 2 + 1)
        below = jnp.stack([near[0], near[1] + down.astype(F32)])
        return above.astype(BF16), below.astype(BF16)

    def later(self, r, up, down):
        up = self.own(r) + up.astype(F32)
        down = self.own(self.n - r) + down.astype(F32)
        return up.astype(BF16), down.astype(BF16)

    def sent(self, pair):
        return moved(pair[0], "z", 1), moved(pair[1], "z", -1)

    def last(self, up, down):
        total = self.own(0) + up.astype(F32) + down.astype(F32)
        mine = lax.dynamic_index_in_dim(total, self.yl, 0, keepdims=False)
        other = lax.dynamic_index_in_dim(total, 1 - self.yl, 0, keepdims=False)
        both = mine + moved(other.astype(BF16), "yl", 1).astype(F32)
        rows = part_of(both, self.c, self.rows_here, 1)
        return rows, moved(part_of(both, 1 - self.c, self.rows_here, 1), "c", 1)


def together(*values):
    return lax.optimization_barrier(values)


def whole_step(
    query_states,
    key_states,
    value_states,
    residual,
    norm_gains,
    lang_labels,
    doc_lengths,
    destinations,
    gate_weight,
    up_weight,
    down_weight,
    out_cotangent,
):
    groups = lax.axis_size(DP)
    my_group = lax.axis_index(DP)
    c, yl = lax.axis_index("c"), lax.axis_index("yl")
    total_units = destinations.shape[0]
    per_group = total_units // groups
    columns = query_states.shape[1]
    width = gate_weight.shape[0]
    tok_group = per_group * UNIT
    rows_here = out_cotangent.shape[0]
    half = width // 2
    gate_t = gate_weight.T
    up_t = up_weight.T

    pair_rows = moved(part_of(out_cotangent, 1 - c, half, 1), "c", 1)
    chip_rows = joined(part_of(out_cotangent, c, half, 1), pair_rows, c, 0)
    run_rows = sent_over_z(chip_rows).reshape(-1, half)
    doc_ids = doc_index(doc_lengths, UNIT)
    unit_index = jnp.arange(total_units, dtype=jnp.int32)
    earlier = unit_index[None, :] < unit_index[:, None]
    same_target = destinations[None, :] == destinations[:, None]
    arrival = jnp.sum((earlier & same_target).astype(jnp.int32), axis=1)
    first_unit = my_group * per_group
    landing_at = jnp.where(destinations == my_group, arrival, -1)
    arrive_ids = jnp.arange(per_group, dtype=jnp.int32)
    landing = landing_at[None, :] == arrive_ids[:, None]
    moved_langs = jnp.sum(landing.astype(jnp.int32) * lang_labels[None, :], axis=1)
    near_x = (lax.axis_index("x") + jnp.arange(groups // 2, dtype=jnp.int32)) % (groups // 2)
    near_y = (lax.axis_index("yh") + jnp.arange(2, dtype=jnp.int32)) % 2
    held_group = (near_x[:, None] * 2 + near_y[None, :]).reshape(-1)
    held_unit = (held_group[:, None] * per_group + arrive_ids[None, :]).reshape(-1)
    held_at = jnp.sum(
        jnp.where(held_unit[:, None] == unit_index[None, :], landing_at[None, :], 0), axis=1
    )
    pick_table = (held_at[None, :] == arrive_ids[:, None]).astype(BF16)
    unit_shape = (per_group, UNIT, columns)
    own_docs = lax.dynamic_slice_in_dim(doc_ids, first_unit, per_group, 0)
    local_mix = attend(
        query_states.reshape(unit_shape),
        key_states.reshape(unit_shape),
        value_states.reshape(unit_shape),
        residual.reshape(unit_shape),
        own_docs,
    )
    pair_mix = jnp.concatenate([local_mix, moved(local_mix, "yh", 1)], axis=0)
    held = jnp.concatenate(
        [
            pair_mix,
            moved(pair_mix, "x", -1),
            moved(pair_mix, "x", 2),
            moved(pair_mix, "x", 1),
        ],
        axis=0,
    )
    stream_cols = (
        jnp.einsum("ju,uic->jic", pick_table, held, preferred_element_type=F32)
        .astype(BF16)
        .reshape(tok_group, columns)
    )

    langs = jnp.arange(norm_gains.shape[0], dtype=jnp.int32)
    unit_gain = jnp.sum(
        jnp.where((moved_langs[:, None] == langs[None, :])[:, :, None], norm_gains[None], 0.0),
        axis=1,
    )
    both_yl = joined(stream_cols[None], moved(stream_cols, "yl", 1)[None], yl, 0)
    run_cols, run_rows, pair_rows = ring_over_z(both_yl, run_rows)
    cot_half = joined(run_rows, pair_rows, yl, 0)
    cot_full = joined(cot_half, moved(cot_half, "c", 1), c, 1)
    cot_own, cot_send = column_parts(cot_full, width // groups)
    run_cols, cot_send = together(run_cols, cot_send)
    cot_arrived = columns_over_x(cot_send)
    nt = (((1,), (1,)), ((), ()))
    tn = (((0,), (0,)), ((), ()))
    grad_hidden = lax.dot_general(down_weight, cot_full, nt, preferred_element_type=F32)
    other_cols = moved(run_cols, "c", 1)
    other_cols, grad_hidden = together(other_cols, grad_hidden)
    stream, scaled, squares = assembled(run_cols, other_cols, unit_gain)
    scaled_own, scaled_send = column_parts(scaled, width // groups)
    scaled_arrived = columns_over_x(scaled_send)
    inv_rms = lax.rsqrt(jnp.sum(squares, axis=1) / width + 1e-05)
    gate_acc = lax.dot_general(gate_t, scaled, nt, preferred_element_type=F32)
    up_acc = lax.dot_general(up_t, scaled, nt, preferred_element_type=F32)
    rms_row = inv_rms[None, :]
    act_gate = rms_row * gate_acc
    act_up = rms_row * up_acc
    sigma = jax.nn.sigmoid(act_gate)
    silu = act_gate * sigma
    hidden = (silu * act_up).astype(BF16)
    scaled_grad = rms_row * grad_hidden
    grad_gate = (scaled_grad * act_up * sigma * (1.0 + act_gate * (1.0 - sigma))).astype(BF16)
    grad_up = (scaled_grad * silu).astype(BF16)
    gate_up = jnp.concatenate([grad_gate, grad_up], axis=0)

    near_hidden = near_over_x(hidden)
    near_gate_up = near_over_x(gate_up)
    out_part = lax.dot_general(hidden, down_weight, tn, preferred_element_type=F32).astype(
        BF16
    )
    back_part = (
        lax.dot_general(grad_gate, gate_t, tn, preferred_element_type=F32)
        + lax.dot_general(grad_up, up_t, tn, preferred_element_type=F32)
    ).astype(BF16)
    sums = RowSums([out_part, back_part], rows_here)
    ring = sums.second(*sums.sent(sums.first()))
    ring, scaled_arrived, cot_arrived = together(ring, scaled_arrived, cot_arrived)
    ring = sums.sent(ring)
    scaled_other = moved(jnp.stack(scaled_arrived), "c", 1)
    cot_other = moved(jnp.stack(cot_arrived), "c", 1)
    ring = sums.later(2, *ring)
    ring, near_hidden, near_gate_up = together(ring, near_hidden, near_gate_up)
    ring = sums.sent(ring)
    far_gate_up = far_over_x(near_gate_up)
    far_hidden = far_over_x(near_hidden)
    ring = sums.later(1, *ring)
    ring, far_hidden, far_gate_up, scaled_other, cot_other = together(
        ring, far_hidden, far_gate_up, scaled_other, cot_other
    )
    ring = sums.sent(ring)
    scaled_keep, scaled_share = column_blocks(scaled_own, scaled_arrived, scaled_other)
    cot_keep, cot_share = column_blocks(cot_own, cot_arrived, cot_other)
    gate_up_all = all_over_x(gate_up, near_gate_up, far_gate_up)
    hidden_all = all_over_x(hidden, near_hidden, far_hidden)
    gate_up_share = pair_share(gate_up_all, scaled_share)
    hidden_share = pair_share(hidden_all, cot_share)
    sums, pair_sums = sums.last(*ring)
    gate_up_grad = weight_grad(gate_up_all, scaled_keep, gate_up_share)
    down_grad = weight_grad(hidden_all, cot_keep, hidden_share)
    hidden_here = gate_weight.shape[1]
    gate_grad = gate_up_grad[:hidden_here].T
    up_grad = gate_up_grad[hidden_here:].T
    layer_out, input_grad = finished(sums, pair_sums, stream, unit_gain, out_cotangent)
    return (layer_out, input_grad, gate_grad, up_grad, down_grad)


def solution(mesh):
    finer = Mesh(mesh.devices.reshape(mesh.shape["dp"] // 2, 2, 2, -1, 2), DP_TENSOR)
    head_cols = P(DP, TENSOR)
    return jax.shard_map(
        whole_step,
        mesh=finer,
        in_specs=(
            head_cols,
            head_cols,
            head_cols,
            head_cols,
            P(),
            P(),
            P(),
            P(),
            P(None, TENSOR),
            P(None, TENSOR),
            P(TENSOR, None),
            P(DP_TENSOR, None),
        ),
        out_specs=(
            P(DP_TENSOR, None),
            P(DP_TENSOR, None),
            P(DP, TENSOR),
            P(DP, TENSOR),
            P(TENSOR, DP),
        ),
        check_vma=False,
    )
```

```python
import math

import jax
import jax.numpy as jnp
from jax import lax
from jax.experimental import pallas as pl
from jax.experimental.pallas import tpu as pltpu
from jax.sharding import Mesh
from jax.sharding import PartitionSpec as P


UNIT = 48
WIN = 24
DP = ("x", "yh")
TENSOR = ("yl", "z", "c")
DP_TENSOR = ("x", "yh", "yl", "z", "c")
F32 = jnp.float32
BF16 = jnp.bfloat16


def moved(array, axis, step):
    n = lax.axis_size(axis)
    return lax.ppermute(array, axis, [(i, (i + step) % n) for i in range(n)])


def joined(mine, other, index, dim):
    return jnp.where(
        index == 0,
        jnp.concatenate([mine, other], axis=dim),
        jnp.concatenate([other, mine], axis=dim),
    )


def sent_over_z(piece):
    n = lax.axis_size("z")
    return lax.all_to_all(jnp.broadcast_to(piece[None], (n, *piece.shape)), "z", 0, 0, tiled=True)


def ring_over_z(piece, rows):
    n = lax.axis_size("z")
    pieces = [piece] * n
    above = below = piece
    for r in range(1, n // 2):
        if r == 2:
            (above, below), rows = lax.optimization_barrier(((above, below), rows))
            pair_rows = moved(rows, "yl", 1)
        above = moved(above, "z", -1)
        below = moved(below, "z", 1)
        pieces[r] = above
        pieces[n - r] = below
    (above, below), pair_rows = lax.optimization_barrier(((above, below), pair_rows))
    far = moved(above[:1], "z", -1), moved(below[1:], "z", 1)
    pieces[n // 2] = jnp.concatenate(far, axis=0)
    return jnp.stack(pieces), rows, pair_rows


def assembled(mine, other, unit_gain):
    n, halves, tokens, lanes = mine.shape
    units = unit_gain.shape[0]
    per_unit = tokens // units
    width = 2 * n * halves * lanes
    run = n // 2

    def kernel(at_ref, *refs):
        mine_refs, other_refs = refs[:run], refs[run : 2 * run]
        gain_ref, stream_ref, scaled_ref, square_ref = refs[2 * run :]

        def write(first_refs, second_refs):
            total = jnp.zeros((tokens, lanes), F32)
            for k in range(2 * run):
                block = (first_refs, second_refs)[k % 2][k // 2][0, 0]
                cols = slice(k * lanes, (k + 1) * lanes)
                stream_ref[:, cols] = block
                wide = block.astype(F32)
                total += wide * wide
                for u in range(units):
                    rows = slice(u * per_unit, (u + 1) * per_unit)
                    scaled_ref[rows, cols] = (wide[rows] * gain_ref[u : u + 1, cols]).astype(BF16)

            @pl.when(pl.program_id(0) == 0)
            def _():
                square_ref[...] = total

            @pl.when(pl.program_id(0) > 0)
            def _():
                square_ref[...] += total

        @pl.when(at_ref[1] == 0)
        def _():
            write(mine_refs, other_refs)

        @pl.when(at_ref[1] == 1)
        def _():
            write(other_refs, mine_refs)

    def piece(k):
        return pl.BlockSpec(
            (1, 1, tokens, lanes),
            lambda i, at: (lax.rem((i % 2) * run + k - at[0] + n, n), i // 2, 0, 0),
        )

    at = jnp.stack([lax.axis_index("z"), lax.axis_index("c")]).astype(jnp.int32)
    wide_block = run * 2 * lanes
    block = pl.BlockSpec((tokens, wide_block), lambda i, at: (0, i))
    return pl.pallas_call(
        kernel,
        grid_spec=pltpu.PrefetchScalarGridSpec(
            num_scalar_prefetch=1,
            grid=(halves * 2,),
            in_specs=[piece(k) for k in range(run)] * 2
            + [pl.BlockSpec((units, wide_block), lambda i, at: (0, i))],
            out_specs=[block, block, pl.BlockSpec((tokens, lanes), lambda i, at: (0, 0))],
        ),
        out_shape=[
            jax.ShapeDtypeStruct((tokens, width), BF16),
            jax.ShapeDtypeStruct((tokens, width), BF16),
            jax.ShapeDtypeStruct((tokens, lanes), F32),
        ],
        compiler_params=pltpu.CompilerParams(vmem_limit_bytes=12 * 2**20),
        name="assembled",
    )(at, *[mine] * run, *[other] * run, unit_gain)


def finished(sums, pair_sums, stream, unit_gain, out_cotangent):
    rows, width = out_cotangent.shape
    half = width // 2
    per_unit = stream.shape[0] // unit_gain.shape[0]

    def kernel(at_ref, sums_ref, pair_ref, stream_ref, gain_ref, cot_ref, out_ref, grad_ref):
        core = at_ref[1]
        gain = gain_ref[pl.ds(at_ref[2], 1), :]

        def work(first_ref, second_ref, row_at):
            kept = stream_ref[...].astype(F32)[row_at : row_at + rows]
            inv = lax.rsqrt(jnp.sum(kept * kept, axis=1, keepdims=True) / width + 1e-05)
            dots = jnp.zeros((rows, 1), F32)
            for k, ref in enumerate((first_ref, second_ref)):
                cols = slice(k * half, (k + 1) * half)
                scaled = (kept[:, cols] * gain[:, cols]).astype(BF16).astype(F32)
                dots += jnp.sum(scaled * ref[1], axis=1, keepdims=True)
            factor = inv * inv / width * dots
            for k, ref in enumerate((first_ref, second_ref)):
                cols = slice(k * half, (k + 1) * half)
                out_ref[:, cols] = (kept[:, cols] + ref[0]).astype(BF16)
                grad_ref[:, cols] = (
                    cot_ref[:, cols].astype(F32)
                    + gain[:, cols] * ref[1]
                    - factor * kept[:, cols]
                ).astype(BF16)

        @pl.when(core == 0)
        def _():
            work(sums_ref, pair_ref, 0)

        @pl.when(core == 1)
        def _():
            work(pair_ref, sums_ref, rows)

    tensor = lax.axis_index(TENSOR)
    at = jnp.stack([tensor // 2, lax.axis_index("c"), tensor * rows // per_unit]).astype(jnp.int32)
    whole = pl.BlockSpec((2, rows, half), lambda i, at: (0, 0, 0))
    out = pl.BlockSpec((rows, width), lambda i, at: (0, 0))
    return pl.pallas_call(
        kernel,
        grid_spec=pltpu.PrefetchScalarGridSpec(
            num_scalar_prefetch=1,
            grid=(1,),
            in_specs=[
                whole,
                whole,
                pl.BlockSpec((2 * rows, width), lambda i, at: (at[0], 0)),
                pl.BlockSpec(unit_gain.shape, lambda i, at: (0, 0)),
                out,
            ],
            out_specs=[out, out],
        ),
        out_shape=[jax.ShapeDtypeStruct((rows, width), BF16)] * 2,
        compiler_params=pltpu.CompilerParams(vmem_limit_bytes=4 * 2**20),
        name="finished",
    )(at, sums, pair_sums, stream, unit_gain, out_cotangent)


def part_of(array, index, size, dim):
    return lax.dynamic_slice_in_dim(array, index * size, size, dim)


def doc_index(doc_lengths, unit_len):
    doc_ends = jnp.cumsum(doc_lengths, axis=1)
    positions = jnp.arange(unit_len, dtype=jnp.int32)
    return jnp.sum((doc_ends[:, None, :] <= positions[None, :, None]).astype(jnp.int32), axis=2)


def attend(query_units, key_units, value_units, resid_units, doc_units):
    head = query_units.shape[2]
    scores = jnp.einsum(
        "uqd,ukd->uqk", query_units, key_units, preferred_element_type=F32
    ) / math.sqrt(head)
    positions = jnp.arange(query_units.shape[1], dtype=jnp.int32)
    distance = positions[:, None] - positions[None, :]
    allowed = (doc_units[:, :, None] == doc_units[:, None, :]) & (
        (distance >= 0) & (distance < WIN)
    )[None]
    scores = jnp.where(allowed, scores, -1e30)
    row_max = jnp.max(scores, axis=2, keepdims=True)
    exp_scores = jnp.exp(scores - row_max)
    attn_probs = (exp_scores / jnp.sum(exp_scores, axis=2, keepdims=True)).astype(BF16)
    mixed = jnp.einsum("uqk,ukd->uqd", attn_probs, value_units, preferred_element_type=F32)
    return (resid_units.astype(F32) + mixed).astype(BF16)


def column_parts(full, width):
    x, c = lax.axis_index("x"), lax.axis_index("c")
    n = lax.axis_size("x")
    block = lambda s, core: part_of(full, 2 * ((x + s) % n) + core, width, 1)
    return (block(0, c), block(0, 1 - c)), (block(1, c), block(n - 1, c), block(2, c))


def columns_over_x(to_send):
    up, down, far = to_send
    return moved(down, "x", -1), moved(up, "x", 1), moved(far, "x", 2)


def column_blocks(own, arrived, other):
    mine = jnp.concatenate([own[0], *arrived], axis=0)
    theirs = jnp.concatenate([own[1], other[0], other[1], other[2]], axis=0)
    same = lax.axis_index("c") == lax.axis_index("yh")
    return jnp.where(same, mine, theirs), jnp.where(same, theirs, mine)


def near_over_x(factor):
    return moved(factor, "x", 1), moved(factor, "x", -1)


def far_over_x(near):
    below, above = near
    half = below.shape[0] // 2
    return moved(below[:half], "x", 1), moved(above[half:], "x", -1)


def all_over_x(factor, near, far):
    below, above = near
    return jnp.concatenate([factor, above, below, jnp.concatenate(far, axis=0)], axis=1)


def shared_part(factor_all, send):
    return jnp.dot(factor_all, send, preferred_element_type=F32).astype(BF16)


class RowSums:
    def __init__(self, parts, rows_here):
        self.rows_here = rows_here
        self.c, self.z = lax.axis_index("c"), lax.axis_index("z")
        self.yl = lax.axis_index("yl")
        self.n = lax.axis_size("z")
        half = parts[0].shape[1] // 2
        shape = (2, self.n, 2 * rows_here, half)
        self.pairs = []
        for part in parts:
            arrived = moved(part_of(part, 1 - self.c, half, 1), "c", 1)
            kept = part_of(part, self.c, half, 1)
            self.pairs += [(kept.reshape(shape), arrived.reshape(shape))]

    def own(self, r):
        at = (self.z + r) % self.n
        pick = lambda a: lax.dynamic_slice_in_dim(a, at, 1, 1)[:, 0].astype(F32)
        return jnp.stack([pick(kept) + pick(arrived) for kept, arrived in self.pairs], axis=1)

    def first(self):
        far = self.own(self.n // 2).astype(BF16)
        return far[0], far[1]

    def second(self, up, down):
        near = self.own(self.n // 2 - 1)
        above = jnp.stack([near[0] + up.astype(F32), near[1]])
        near = self.own(self.n - self.n // 2 + 1)
        below = jnp.stack([near[0], near[1] + down.astype(F32)])
        return above.astype(BF16), below.astype(BF16)

    def later(self, r, up, down):
        up = self.own(r) + up.astype(F32)
        down = self.own(self.n - r) + down.astype(F32)
        return up.astype(BF16), down.astype(BF16)

    def sent(self, pair):
        return moved(pair[0], "z", 1), moved(pair[1], "z", -1)

    def last(self, up, down):
        total = self.own(0) + up.astype(F32) + down.astype(F32)
        mine = lax.dynamic_index_in_dim(total, self.yl, 0, keepdims=False)
        other = lax.dynamic_index_in_dim(total, 1 - self.yl, 0, keepdims=False)
        both = mine + moved(other.astype(BF16), "yl", 1).astype(F32)
        rows = part_of(both, self.c, self.rows_here, 1)
        return rows, moved(part_of(both, 1 - self.c, self.rows_here, 1), "c", 1)


def together(*values):
    return lax.optimization_barrier(values)


def whole_step(
    query_states,
    key_states,
    value_states,
    residual,
    norm_gains,
    lang_labels,
    doc_lengths,
    destinations,
    gate_weight,
    up_weight,
    down_weight,
    out_cotangent,
):
    groups = lax.axis_size(DP)
    my_group = lax.axis_index(DP)
    c, yl = lax.axis_index("c"), lax.axis_index("yl")
    total_units = destinations.shape[0]
    per_group = total_units // groups
    columns = query_states.shape[1]
    width = gate_weight.shape[0]
    tok_group = per_group * UNIT
    rows_here = out_cotangent.shape[0]
    half = width // 2
    gate_t = gate_weight.T
    up_t = up_weight.T

    pair_rows = moved(part_of(out_cotangent, 1 - c, half, 1), "c", 1)
    chip_rows = joined(part_of(out_cotangent, c, half, 1), pair_rows, c, 0)
    run_rows = sent_over_z(chip_rows).reshape(-1, half)
    doc_ids = doc_index(doc_lengths, UNIT)
    unit_index = jnp.arange(total_units, dtype=jnp.int32)
    earlier = unit_index[None, :] < unit_index[:, None]
    same_target = destinations[None, :] == destinations[:, None]
    arrival = jnp.sum((earlier & same_target).astype(jnp.int32), axis=1)
    first_unit = my_group * per_group
    landing_at = jnp.where(destinations == my_group, arrival, -1)
    arrive_ids = jnp.arange(per_group, dtype=jnp.int32)
    landing = landing_at[None, :] == arrive_ids[:, None]
    moved_langs = jnp.sum(landing.astype(jnp.int32) * lang_labels[None, :], axis=1)
    near_x = (lax.axis_index("x") + jnp.arange(groups // 2, dtype=jnp.int32)) % (groups // 2)
    near_y = (lax.axis_index("yh") + jnp.arange(2, dtype=jnp.int32)) % 2
    held_group = (near_x[:, None] * 2 + near_y[None, :]).reshape(-1)
    held_unit = (held_group[:, None] * per_group + arrive_ids[None, :]).reshape(-1)
    held_at = jnp.sum(
        jnp.where(held_unit[:, None] == unit_index[None, :], landing_at[None, :], 0), axis=1
    )
    pick_table = (held_at[None, :] == arrive_ids[:, None]).astype(BF16)
    unit_shape = (per_group, UNIT, columns)
    own_docs = lax.dynamic_slice_in_dim(doc_ids, first_unit, per_group, 0)
    local_mix = attend(
        query_states.reshape(unit_shape),
        key_states.reshape(unit_shape),
        value_states.reshape(unit_shape),
        residual.reshape(unit_shape),
        own_docs,
    )
    pair_mix = jnp.concatenate([local_mix, moved(local_mix, "yh", 1)], axis=0)
    others = [moved(pair_mix, "x", step) for step in (-1, 2, 1)]
    held = jnp.concatenate([pair_mix, *others], axis=0)
    stream_cols = (
        jnp.einsum("ju,uic->jic", pick_table, held, preferred_element_type=F32)
        .astype(BF16)
        .reshape(tok_group, columns)
    )

    langs = jnp.arange(norm_gains.shape[0], dtype=jnp.int32)
    unit_gain = jnp.sum(
        jnp.where((moved_langs[:, None] == langs[None, :])[:, :, None], norm_gains[None], 0.0),
        axis=1,
    )
    both_yl = joined(stream_cols[None], moved(stream_cols, "yl", 1)[None], yl, 0)
    run_cols, run_rows, pair_rows = ring_over_z(both_yl, run_rows)
    cot_half = joined(run_rows, pair_rows, yl, 0)
    cot_full = joined(cot_half, moved(cot_half, "c", 1), c, 1)
    cot_own, cot_send = column_parts(cot_full, width // groups)
    run_cols, cot_send = together(run_cols, cot_send)
    cot_arrived = columns_over_x(cot_send)
    nt = (((1,), (1,)), ((), ()))
    tn = (((0,), (0,)), ((), ()))
    grad_hidden = lax.dot_general(down_weight, cot_full, nt, preferred_element_type=F32)
    other_cols = moved(run_cols, "c", 1)
    other_cols, grad_hidden = together(other_cols, grad_hidden)
    stream, scaled, squares = assembled(run_cols, other_cols, unit_gain)
    scaled_own, scaled_send = column_parts(scaled, width // groups)
    scaled_arrived = columns_over_x(scaled_send)
    inv_rms = lax.rsqrt(jnp.sum(squares, axis=1) / width + 1e-05)
    gate_acc = lax.dot_general(gate_t, scaled, nt, preferred_element_type=F32)
    up_acc = lax.dot_general(up_t, scaled, nt, preferred_element_type=F32)
    rms_row = inv_rms[None, :]
    act_gate = rms_row * gate_acc
    act_up = rms_row * up_acc
    sigma = jax.nn.sigmoid(act_gate)
    silu = act_gate * sigma
    hidden = (silu * act_up).astype(BF16)
    scaled_grad = rms_row * grad_hidden
    grad_gate = (scaled_grad * act_up * sigma * (1.0 + act_gate * (1.0 - sigma))).astype(BF16)
    grad_up = (scaled_grad * silu).astype(BF16)
    gate_up = jnp.concatenate([grad_gate, grad_up], axis=0)

    near_hidden = near_over_x(hidden)
    near_gate_up = near_over_x(gate_up)
    out_part = lax.dot_general(hidden, down_weight, tn, preferred_element_type=F32).astype(
        BF16
    )
    back_part = (
        lax.dot_general(grad_gate, gate_t, tn, preferred_element_type=F32)
        + lax.dot_general(grad_up, up_t, tn, preferred_element_type=F32)
    ).astype(BF16)
    sums = RowSums([out_part, back_part], rows_here)
    ring = sums.second(*sums.sent(sums.first()))
    ring, scaled_arrived, cot_arrived, near_hidden, near_gate_up = together(
        ring, scaled_arrived, cot_arrived, near_hidden, near_gate_up
    )
    ring = sums.sent(ring)
    far_gate_up = far_over_x(near_gate_up)
    scaled_other = moved(jnp.stack(scaled_arrived), "c", 1)
    far_hidden = far_over_x(near_hidden)
    cot_other = moved(jnp.stack(cot_arrived), "c", 1)
    ring = sums.later(2, *ring)
    ring, far_hidden, far_gate_up, scaled_other, cot_other = together(
        ring, far_hidden, far_gate_up, scaled_other, cot_other
    )
    ring = sums.sent(ring)
    scaled_keep, scaled_share = column_blocks(scaled_own, scaled_arrived, scaled_other)
    cot_keep, cot_share = column_blocks(cot_own, cot_arrived, cot_other)
    gate_up_all = all_over_x(gate_up, near_gate_up, far_gate_up)
    hidden_all = all_over_x(hidden, near_hidden, far_hidden)
    gate_up_sent = shared_part(gate_up_all, scaled_share)
    hidden_sent = shared_part(hidden_all, cot_share)
    gate_up_share = moved(gate_up_sent, "yh", 1)
    hidden_share = moved(hidden_sent, "yh", 1)
    ring = sums.sent(sums.later(1, *ring))
    gate_up_kept = jnp.dot(gate_up_all, scaled_keep, preferred_element_type=F32)
    hidden_kept = jnp.dot(hidden_all, cot_keep, preferred_element_type=F32)
    ring, gate_up_kept, hidden_kept = together(ring, gate_up_kept, hidden_kept)
    sums, pair_sums = sums.last(*ring)
    gate_up_grad = (gate_up_kept + gate_up_share.astype(F32)).astype(BF16)
    down_grad = (hidden_kept + hidden_share.astype(F32)).astype(BF16)
    hidden_here = gate_weight.shape[1]
    gate_grad = gate_up_grad[:hidden_here].T
    up_grad = gate_up_grad[hidden_here:].T
    layer_out, input_grad = finished(sums, pair_sums, stream, unit_gain, out_cotangent)
    return (layer_out, input_grad, gate_grad, up_grad, down_grad)


def solution(mesh):
    finer = Mesh(mesh.devices.reshape(mesh.shape["dp"] // 2, 2, 2, -1, 2), DP_TENSOR)
    head_cols = P(DP, TENSOR)
    return jax.shard_map(
        whole_step,
        mesh=finer,
        in_specs=(
            head_cols,
            head_cols,
            head_cols,
            head_cols,
            P(),
            P(),
            P(),
            P(),
            P(None, TENSOR),
            P(None, TENSOR),
            P(TENSOR, None),
            P(DP_TENSOR, None),
        ),
        out_specs=(
            P(DP_TENSOR, None),
            P(DP_TENSOR, None),
            P(DP, TENSOR),
            P(DP, TENSOR),
            P(TENSOR, DP),
        ),
        check_vma=False,
    )
```

```python
import math

import jax
import jax.numpy as jnp
from jax import lax
from jax.experimental import pallas as pl
from jax.experimental.pallas import tpu as pltpu
from jax.sharding import Mesh
from jax.sharding import PartitionSpec as P


UNIT = 48
WIN = 24
DP = ("x", "yh")
TENSOR = ("yl", "z", "c")
DP_TENSOR = ("x", "yh", "yl", "z", "c")
F32 = jnp.float32
BF16 = jnp.bfloat16


def moved(array, axis, step):
    n = lax.axis_size(axis)
    return lax.ppermute(array, axis, [(i, (i + step) % n) for i in range(n)])


def joined(mine, other, index, dim):
    return jnp.where(
        index == 0,
        jnp.concatenate([mine, other], axis=dim),
        jnp.concatenate([other, mine], axis=dim),
    )


def sent_over_z(piece):
    n = lax.axis_size("z")
    return lax.all_to_all(jnp.broadcast_to(piece[None], (n, *piece.shape)), "z", 0, 0, tiled=True)


def ring_over_z(piece):
    n = lax.axis_size("z")
    pieces = [piece] * n
    above = below = piece
    for r in range(1, n // 2):
        above = moved(above, "z", -1)
        below = moved(below, "z", 1)
        pieces[r] = above
        pieces[n - r] = below
    far = moved(above[:1], "z", -1), moved(below[1:], "z", 1)
    pieces[n // 2] = jnp.concatenate(far, axis=0)
    return jnp.stack(pieces)


def assembled(mine, other, unit_gain):
    n, halves, tokens, lanes = mine.shape
    units = unit_gain.shape[0]
    per_unit = tokens // units
    width = 2 * n * halves * lanes
    run = n // 2

    def kernel(at_ref, *refs):
        mine_refs, other_refs = refs[:run], refs[run : 2 * run]
        gain_ref, stream_ref, scaled_ref, square_ref = refs[2 * run :]

        def write(first_refs, second_refs):
            total = jnp.zeros((tokens, lanes), F32)
            for k in range(2 * run):
                block = (first_refs, second_refs)[k % 2][k // 2][0, 0]
                cols = slice(k * lanes, (k + 1) * lanes)
                stream_ref[:, cols] = block
                wide = block.astype(F32)
                total += wide * wide
                for u in range(units):
                    rows = slice(u * per_unit, (u + 1) * per_unit)
                    scaled_ref[rows, cols] = (wide[rows] * gain_ref[u : u + 1, cols]).astype(BF16)

            @pl.when(pl.program_id(0) == 0)
            def _():
                square_ref[...] = total

            @pl.when(pl.program_id(0) > 0)
            def _():
                square_ref[...] += total

        @pl.when(at_ref[1] == 0)
        def _():
            write(mine_refs, other_refs)

        @pl.when(at_ref[1] == 1)
        def _():
            write(other_refs, mine_refs)

    def piece(k):
        return pl.BlockSpec(
            (1, 1, tokens, lanes),
            lambda i, at: (lax.rem((i % 2) * run + k - at[0] + n, n), i // 2, 0, 0),
        )

    at = jnp.stack([lax.axis_index("z"), lax.axis_index("c")]).astype(jnp.int32)
    wide_block = run * 2 * lanes
    block = pl.BlockSpec((tokens, wide_block), lambda i, at: (0, i))
    return pl.pallas_call(
        kernel,
        grid_spec=pltpu.PrefetchScalarGridSpec(
            num_scalar_prefetch=1,
            grid=(halves * 2,),
            in_specs=[piece(k) for k in range(run)] * 2
            + [pl.BlockSpec((units, wide_block), lambda i, at: (0, i))],
            out_specs=[block, block, pl.BlockSpec((tokens, lanes), lambda i, at: (0, 0))],
        ),
        out_shape=[
            pltpu.HBM((tokens, width), BF16),
            pltpu.HBM((tokens, width), BF16),
            jax.ShapeDtypeStruct((tokens, lanes), F32),
        ],
        compiler_params=pltpu.CompilerParams(vmem_limit_bytes=12 * 2**20),
        name="assembled",
    )(at, *[mine] * run, *[other] * run, unit_gain)


def finished(sums, pair_sums, stream, unit_gain, out_cotangent):
    rows, width = out_cotangent.shape
    half = width // 2
    per_unit = stream.shape[0] // unit_gain.shape[0]

    def kernel(at_ref, sums_ref, pair_ref, stream_ref, gain_ref, cot_ref, out_ref, grad_ref):
        core = at_ref[1]
        gain = gain_ref[pl.ds(at_ref[2], 1), :]

        def work(first_ref, second_ref, row_at):
            kept = stream_ref[...].astype(F32)[row_at : row_at + rows]
            inv = lax.rsqrt(jnp.sum(kept * kept, axis=1, keepdims=True) / width + 1e-05)
            dots = jnp.zeros((rows, 1), F32)
            for k, ref in enumerate((first_ref, second_ref)):
                cols = slice(k * half, (k + 1) * half)
                scaled = (kept[:, cols] * gain[:, cols]).astype(BF16).astype(F32)
                dots += jnp.sum(scaled * ref[1], axis=1, keepdims=True)
            factor = inv * inv / width * dots
            for k, ref in enumerate((first_ref, second_ref)):
                cols = slice(k * half, (k + 1) * half)
                out_ref[:, cols] = (kept[:, cols] + ref[0]).astype(BF16)
                grad_ref[:, cols] = (
                    cot_ref[:, cols].astype(F32)
                    + gain[:, cols] * ref[1]
                    - factor * kept[:, cols]
                ).astype(BF16)

        @pl.when(core == 0)
        def _():
            work(sums_ref, pair_ref, 0)

        @pl.when(core == 1)
        def _():
            work(pair_ref, sums_ref, rows)

    tensor = lax.axis_index(TENSOR)
    at = jnp.stack([tensor // 2, lax.axis_index("c"), tensor * rows // per_unit]).astype(jnp.int32)
    whole = pl.BlockSpec((2, rows, half), lambda i, at: (0, 0, 0))
    out = pl.BlockSpec((rows, width), lambda i, at: (0, 0))
    return pl.pallas_call(
        kernel,
        grid_spec=pltpu.PrefetchScalarGridSpec(
            num_scalar_prefetch=1,
            grid=(1,),
            in_specs=[
                whole,
                whole,
                pl.BlockSpec((2 * rows, width), lambda i, at: (at[0], 0)),
                pl.BlockSpec(unit_gain.shape, lambda i, at: (0, 0)),
                out,
            ],
            out_specs=[out, out],
        ),
        out_shape=[jax.ShapeDtypeStruct((rows, width), BF16)] * 2,
        compiler_params=pltpu.CompilerParams(vmem_limit_bytes=4 * 2**20),
        name="finished",
    )(at, sums, pair_sums, stream, unit_gain, out_cotangent)


def part_of(array, index, size, dim):
    return lax.dynamic_slice_in_dim(array, index * size, size, dim)


def doc_index(doc_lengths, unit_len):
    doc_ends = jnp.cumsum(doc_lengths, axis=1)
    positions = jnp.arange(unit_len, dtype=jnp.int32)
    return jnp.sum((doc_ends[:, None, :] <= positions[None, :, None]).astype(jnp.int32), axis=2)


def attend(query_units, key_units, value_units, resid_units, doc_units):
    head = query_units.shape[2]
    scores = jnp.einsum(
        "uqd,ukd->uqk", query_units, key_units, preferred_element_type=F32
    ) / math.sqrt(head)
    positions = jnp.arange(query_units.shape[1], dtype=jnp.int32)
    distance = positions[:, None] - positions[None, :]
    allowed = (doc_units[:, :, None] == doc_units[:, None, :]) & (
        (distance >= 0) & (distance < WIN)
    )[None]
    scores = jnp.where(allowed, scores, -1e30)
    row_max = jnp.max(scores, axis=2, keepdims=True)
    exp_scores = jnp.exp(scores - row_max)
    attn_probs = (exp_scores / jnp.sum(exp_scores, axis=2, keepdims=True)).astype(BF16)
    mixed = jnp.einsum("uqk,ukd->uqd", attn_probs, value_units, preferred_element_type=F32)
    return (resid_units.astype(F32) + mixed).astype(BF16)


def column_parts(full, width):
    x, c = lax.axis_index("x"), lax.axis_index("c")
    n = lax.axis_size("x")
    block = lambda s, core: part_of(full, 2 * ((x + s) % n) + core, width, 1)
    return (block(0, c), block(0, 1 - c)), (block(1, c), block(n - 1, c), block(2, c))


def columns_over_x(to_send):
    up, down, far = to_send
    return moved(down, "x", -1), moved(up, "x", 1), moved(far, "x", 2)


def column_blocks(own, arrived, other):
    mine = jnp.concatenate([own[0], *arrived], axis=0)
    theirs = jnp.concatenate([own[1], other[0], other[1], other[2]], axis=0)
    same = lax.axis_index("c") == lax.axis_index("yh")
    return jnp.where(same, mine, theirs), jnp.where(same, theirs, mine)


def sent_over_x(factor):
    return [moved(factor, "x", step) for step in (-1, 1, 2)]


def all_over_x(factor, others):
    return jnp.concatenate([factor, *others], axis=1)


def shared_part(factor_all, send):
    return jnp.dot(factor_all, send, preferred_element_type=F32).astype(BF16)


class RowSums:
    def __init__(self, parts, rows_here):
        self.rows_here = rows_here
        self.c, self.z = lax.axis_index("c"), lax.axis_index("z")
        self.yl = lax.axis_index("yl")
        self.n = lax.axis_size("z")
        half = parts[0].shape[1] // 2
        shape = (2, self.n, 2 * rows_here, half)
        self.pairs = []
        for part in parts:
            arrived = moved(part_of(part, 1 - self.c, half, 1), "c", 1)
            kept = part_of(part, self.c, half, 1)
            self.pairs += [(kept.reshape(shape), arrived.reshape(shape))]

    def own(self, r):
        at = (self.z + r) % self.n
        pick = lambda a: lax.dynamic_slice_in_dim(a, at, 1, 1)[:, 0].astype(F32)
        return jnp.stack([pick(kept) + pick(arrived) for kept, arrived in self.pairs], axis=1)

    def first(self):
        far = self.own(self.n // 2).astype(BF16)
        return far[0], far[1]

    def second(self, up, down):
        near = self.own(self.n // 2 - 1)
        above = jnp.stack([near[0] + up.astype(F32), near[1]])
        near = self.own(self.n - self.n // 2 + 1)
        below = jnp.stack([near[0], near[1] + down.astype(F32)])
        return above.astype(BF16), below.astype(BF16)

    def later(self, r, up, down):
        up = self.own(r) + up.astype(F32)
        down = self.own(self.n - r) + down.astype(F32)
        return up.astype(BF16), down.astype(BF16)

    def sent(self, pair):
        return moved(pair[0], "z", 1), moved(pair[1], "z", -1)

    def last(self, up, down):
        total = self.own(0) + up.astype(F32) + down.astype(F32)
        mine = lax.dynamic_index_in_dim(total, self.yl, 0, keepdims=False)
        other = lax.dynamic_index_in_dim(total, 1 - self.yl, 0, keepdims=False)
        pair = moved(other.astype(BF16), "yl", 1)
        both = mine + pair.astype(F32)
        rows = part_of(both, self.c, self.rows_here, 1)
        return rows, moved(part_of(both, 1 - self.c, self.rows_here, 1), "c", 1)


def together(*values):
    return lax.optimization_barrier(values)


def whole_step(
    query_states,
    key_states,
    value_states,
    residual,
    norm_gains,
    lang_labels,
    doc_lengths,
    destinations,
    gate_weight,
    up_weight,
    down_weight,
    out_cotangent,
):
    groups = lax.axis_size(DP)
    my_group = lax.axis_index(DP)
    c, yl = lax.axis_index("c"), lax.axis_index("yl")
    total_units = destinations.shape[0]
    per_group = total_units // groups
    columns = query_states.shape[1]
    width = gate_weight.shape[0]
    tok_group = per_group * UNIT
    rows_here = out_cotangent.shape[0]
    half = width // 2
    gate_t = gate_weight.T
    up_t = up_weight.T

    pair_rows = moved(part_of(out_cotangent, 1 - c, half, 1), "c", 1)
    chip_rows = joined(part_of(out_cotangent, c, half, 1), pair_rows, c, 0)
    run_rows = sent_over_z(chip_rows).reshape(-1, half)
    doc_ids = doc_index(doc_lengths, UNIT)
    unit_index = jnp.arange(total_units, dtype=jnp.int32)
    earlier = unit_index[None, :] < unit_index[:, None]
    same_target = destinations[None, :] == destinations[:, None]
    arrival = jnp.sum((earlier & same_target).astype(jnp.int32), axis=1)
    first_unit = my_group * per_group
    landing_at = jnp.where(destinations == my_group, arrival, -1)
    arrive_ids = jnp.arange(per_group, dtype=jnp.int32)
    landing = landing_at[None, :] == arrive_ids[:, None]
    moved_langs = jnp.sum(landing.astype(jnp.int32) * lang_labels[None, :], axis=1)
    near_x = (lax.axis_index("x") + jnp.arange(groups // 2, dtype=jnp.int32)) % (groups // 2)
    near_y = (lax.axis_index("yh") + jnp.arange(2, dtype=jnp.int32)) % 2
    held_group = (near_x[:, None] * 2 + near_y[None, :]).reshape(-1)
    held_unit = (held_group[:, None] * per_group + arrive_ids[None, :]).reshape(-1)
    held_at = jnp.sum(
        jnp.where(held_unit[:, None] == unit_index[None, :], landing_at[None, :], 0), axis=1
    )
    pick_table = (held_at[None, :] == arrive_ids[:, None]).astype(BF16)
    unit_shape = (per_group, UNIT, columns)
    own_docs = lax.dynamic_slice_in_dim(doc_ids, first_unit, per_group, 0)
    local_mix = attend(
        query_states.reshape(unit_shape),
        key_states.reshape(unit_shape),
        value_states.reshape(unit_shape),
        residual.reshape(unit_shape),
        own_docs,
    )
    pair_mix = jnp.concatenate([local_mix, moved(local_mix, "yh", 1)], axis=0)
    others = [moved(pair_mix, "x", step) for step in (-1, 2, 1)]
    held = jnp.concatenate([pair_mix, *others], axis=0)
    stream_cols = (
        jnp.einsum("ju,uic->jic", pick_table, held, preferred_element_type=F32)
        .astype(BF16)
        .reshape(tok_group, columns)
    )

    langs = jnp.arange(norm_gains.shape[0], dtype=jnp.int32)
    unit_gain = jnp.sum(
        jnp.where((moved_langs[:, None] == langs[None, :])[:, :, None], norm_gains[None], 0.0),
        axis=1,
    )
    both_yl = joined(stream_cols[None], moved(stream_cols, "yl", 1)[None], yl, 0)
    run_cols = ring_over_z(both_yl)
    pair_rows = moved(run_rows, "yl", 1)
    cot_half = joined(run_rows, pair_rows, yl, 0)
    pair_half = moved(cot_half, "c", 1)
    cot_full = joined(cot_half, pair_half, c, 1)
    cot_own, cot_send = column_parts(cot_full, width // groups)
    cot_arrived = columns_over_x(cot_send)
    nt = (((1,), (1,)), ((), ()))
    tn = (((0,), (0,)), ((), ()))
    grad_hidden = lax.dot_general(down_weight, cot_full, nt, preferred_element_type=F32)
    other_cols = moved(run_cols, "c", 1)
    stream, scaled, squares = assembled(run_cols, other_cols, unit_gain)
    scaled_own, scaled_send = column_parts(scaled, width // groups)
    scaled_arrived = columns_over_x(scaled_send)
    inv_rms = lax.rsqrt(jnp.sum(squares, axis=1) / width + 1e-05)
    gate_acc = lax.dot_general(gate_t, scaled, nt, preferred_element_type=F32)
    up_acc = lax.dot_general(up_t, scaled, nt, preferred_element_type=F32)
    rms_row = inv_rms[None, :]
    act_gate = rms_row * gate_acc
    act_up = rms_row * up_acc
    sigma = jax.nn.sigmoid(act_gate)
    silu = act_gate * sigma
    hidden = (silu * act_up).astype(BF16)
    scaled_grad = rms_row * grad_hidden
    grad_gate = (scaled_grad * act_up * sigma * (1.0 + act_gate * (1.0 - sigma))).astype(BF16)
    grad_up = (scaled_grad * silu).astype(BF16)
    gate_up = jnp.concatenate([grad_gate, grad_up], axis=0)

    other_hidden = sent_over_x(hidden)
    other_gate_up = sent_over_x(gate_up)
    out_part = lax.dot_general(hidden, down_weight, tn, preferred_element_type=F32).astype(
        BF16
    )
    back_part = (
        lax.dot_general(grad_gate, gate_t, tn, preferred_element_type=F32)
        + lax.dot_general(grad_up, up_t, tn, preferred_element_type=F32)
    ).astype(BF16)
    sums = RowSums([out_part, back_part], rows_here)
    ring = sums.first()
    ring = sums.sent(ring)
    ring = sums.second(*ring)
    ring = sums.sent(ring)
    scaled_other = moved(jnp.stack(scaled_arrived), "c", 1)
    cot_other = moved(jnp.stack(cot_arrived), "c", 1)
    ring = sums.later(2, *ring)
    ring = sums.sent(ring)
    scaled_keep, scaled_share = column_blocks(scaled_own, scaled_arrived, scaled_other)
    cot_keep, cot_share = column_blocks(cot_own, cot_arrived, cot_other)
    gate_up_all = all_over_x(gate_up, other_gate_up)
    hidden_all = all_over_x(hidden, other_hidden)
    gate_up_sent = shared_part(gate_up_all, scaled_share)
    hidden_sent = shared_part(hidden_all, cot_share)
    gate_up_share = moved(gate_up_sent, "yh", 1)
    hidden_share = moved(hidden_sent, "yh", 1)
    ring = sums.later(1, *ring)
    ring = sums.sent(ring)
    gate_up_kept = jnp.dot(gate_up_all, scaled_keep, preferred_element_type=F32)
    hidden_kept = jnp.dot(hidden_all, cot_keep, preferred_element_type=F32)
    gate_up_kept, hidden_kept = together(gate_up_kept, hidden_kept)
    sums, pair_sums = sums.last(*ring)
    gate_up_grad = (gate_up_kept + gate_up_share.astype(F32)).astype(BF16)
    down_grad = (hidden_kept + hidden_share.astype(F32)).astype(BF16)
    hidden_here = gate_weight.shape[1]
    gate_grad = gate_up_grad[:hidden_here].T
    up_grad = gate_up_grad[hidden_here:].T
    layer_out, input_grad = finished(sums, pair_sums, stream, unit_gain, out_cotangent)
    return (layer_out, input_grad, gate_grad, up_grad, down_grad)


def solution(mesh):
    finer = Mesh(mesh.devices.reshape(mesh.shape["dp"] // 2, 2, 2, -1, 2), DP_TENSOR)
    head_cols = P(DP, TENSOR)
    return jax.shard_map(
        whole_step,
        mesh=finer,
        in_specs=(
            head_cols,
            head_cols,
            head_cols,
            head_cols,
            P(),
            P(),
            P(),
            P(),
            P(None, TENSOR),
            P(None, TENSOR),
            P(TENSOR, None),
            P(DP_TENSOR, None),
        ),
        out_specs=(
            P(DP_TENSOR, None),
            P(DP_TENSOR, None),
            P(DP, TENSOR),
            P(DP, TENSOR),
            P(TENSOR, DP),
        ),
        check_vma=False,
    )
```

```python
import math

import jax
import jax.numpy as jnp
from jax import lax
from jax.experimental import pallas as pl
from jax.experimental.pallas import tpu as pltpu
from jax.sharding import Mesh
from jax.sharding import PartitionSpec as P


UNIT = 48
WIN = 24
DP = ("x", "yh")
TENSOR = ("yl", "z", "c")
DP_TENSOR = ("x", "yh", "yl", "z", "c")
F32 = jnp.float32
BF16 = jnp.bfloat16


def moved(array, axis, step):
    n = lax.axis_size(axis)
    return lax.ppermute(array, axis, [(i, (i + step) % n) for i in range(n)])


def joined(mine, other, index, dim):
    return jnp.where(
        index == 0,
        jnp.concatenate([mine, other], axis=dim),
        jnp.concatenate([other, mine], axis=dim),
    )


def sent_over_z(piece):
    n = lax.axis_size("z")
    return lax.all_to_all(jnp.broadcast_to(piece[None], (n, *piece.shape)), "z", 0, 0, tiled=True)


def ring_over_z(piece):
    n = lax.axis_size("z")
    pieces = [piece] * n
    above = below = piece
    for r in range(1, n // 2):
        above = moved(above, "z", -1)
        below = moved(below, "z", 1)
        pieces[r] = above
        pieces[n - r] = below
    far = moved(above[:1], "z", -1), moved(below[1:], "z", 1)
    pieces[n // 2] = jnp.concatenate(far, axis=0)
    return jnp.stack(pieces)


def assembled(mine, other, unit_gain):
    n, halves, tokens, lanes = mine.shape
    units = unit_gain.shape[0]
    per_unit = tokens // units
    width = 2 * n * halves * lanes
    run = n // 2

    def kernel(at_ref, *refs):
        mine_refs, other_refs = refs[:run], refs[run : 2 * run]
        gain_ref, stream_ref, scaled_ref, square_ref = refs[2 * run :]

        def write(first_refs, second_refs):
            total = jnp.zeros((tokens, lanes), F32)
            for k in range(2 * run):
                block = (first_refs, second_refs)[k % 2][k // 2][0, 0]
                cols = slice(k * lanes, (k + 1) * lanes)
                stream_ref[:, cols] = block
                wide = block.astype(F32)
                total += wide * wide
                for u in range(units):
                    rows = slice(u * per_unit, (u + 1) * per_unit)
                    scaled_ref[rows, cols] = (wide[rows] * gain_ref[u : u + 1, cols]).astype(BF16)

            @pl.when(pl.program_id(0) == 0)
            def _():
                square_ref[...] = total

            @pl.when(pl.program_id(0) > 0)
            def _():
                square_ref[...] += total

        @pl.when(at_ref[1] == 0)
        def _():
            write(mine_refs, other_refs)

        @pl.when(at_ref[1] == 1)
        def _():
            write(other_refs, mine_refs)

    def piece(k):
        return pl.BlockSpec(
            (1, 1, tokens, lanes),
            lambda i, at: (lax.rem((i % 2) * run + k - at[0] + n, n), i // 2, 0, 0),
        )

    at = jnp.stack([lax.axis_index("z"), lax.axis_index("c")]).astype(jnp.int32)
    wide_block = run * 2 * lanes
    block = pl.BlockSpec((tokens, wide_block), lambda i, at: (0, i))
    return pl.pallas_call(
        kernel,
        grid_spec=pltpu.PrefetchScalarGridSpec(
            num_scalar_prefetch=1,
            grid=(halves * 2,),
            in_specs=[piece(k) for k in range(run)] * 2
            + [pl.BlockSpec((units, wide_block), lambda i, at: (0, i))],
            out_specs=[block, block, pl.BlockSpec((tokens, lanes), lambda i, at: (0, 0))],
        ),
        out_shape=[
            pltpu.HBM((tokens, width), BF16),
            pltpu.HBM((tokens, width), BF16),
            jax.ShapeDtypeStruct((tokens, lanes), F32),
        ],
        compiler_params=pltpu.CompilerParams(vmem_limit_bytes=12 * 2**20),
        name="assembled",
    )(at, *[mine] * run, *[other] * run, unit_gain)


def finished(sums, pair_sums, stream, unit_gain, out_cotangent):
    rows, width = out_cotangent.shape
    half = width // 2
    per_unit = stream.shape[0] // unit_gain.shape[0]

    def kernel(at_ref, sums_ref, pair_ref, stream_ref, gain_ref, cot_ref, out_ref, grad_ref):
        core = at_ref[1]
        gain = gain_ref[pl.ds(at_ref[2], 1), :]

        def work(first_ref, second_ref, row_at):
            kept = stream_ref[...].astype(F32)[row_at : row_at + rows]
            inv = lax.rsqrt(jnp.sum(kept * kept, axis=1, keepdims=True) / width + 1e-05)
            dots = jnp.zeros((rows, 1), F32)
            for k, ref in enumerate((first_ref, second_ref)):
                cols = slice(k * half, (k + 1) * half)
                scaled = (kept[:, cols] * gain[:, cols]).astype(BF16).astype(F32)
                dots += jnp.sum(scaled * ref[1], axis=1, keepdims=True)
            factor = inv * inv / width * dots
            for k, ref in enumerate((first_ref, second_ref)):
                cols = slice(k * half, (k + 1) * half)
                out_ref[:, cols] = (kept[:, cols] + ref[0]).astype(BF16)
                grad_ref[:, cols] = (
                    cot_ref[:, cols].astype(F32)
                    + gain[:, cols] * ref[1]
                    - factor * kept[:, cols]
                ).astype(BF16)

        @pl.when(core == 0)
        def _():
            work(sums_ref, pair_ref, 0)

        @pl.when(core == 1)
        def _():
            work(pair_ref, sums_ref, rows)

    tensor = lax.axis_index(TENSOR)
    at = jnp.stack([tensor // 2, lax.axis_index("c"), tensor * rows // per_unit]).astype(jnp.int32)
    whole = pl.BlockSpec((2, rows, half), lambda i, at: (0, 0, 0))
    out = pl.BlockSpec((rows, width), lambda i, at: (0, 0))
    return pl.pallas_call(
        kernel,
        grid_spec=pltpu.PrefetchScalarGridSpec(
            num_scalar_prefetch=1,
            grid=(1,),
            in_specs=[
                whole,
                whole,
                pl.BlockSpec((2 * rows, width), lambda i, at: (at[0], 0)),
                pl.BlockSpec(unit_gain.shape, lambda i, at: (0, 0)),
                out,
            ],
            out_specs=[out, out],
        ),
        out_shape=[jax.ShapeDtypeStruct((rows, width), BF16)] * 2,
        compiler_params=pltpu.CompilerParams(vmem_limit_bytes=4 * 2**20),
        name="finished",
    )(at, sums, pair_sums, stream, unit_gain, out_cotangent)


def part_of(array, index, size, dim):
    return lax.dynamic_slice_in_dim(array, index * size, size, dim)


def doc_index(doc_lengths, unit_len):
    doc_ends = jnp.cumsum(doc_lengths, axis=1)
    positions = jnp.arange(unit_len, dtype=jnp.int32)
    return jnp.sum((doc_ends[:, None, :] <= positions[None, :, None]).astype(jnp.int32), axis=2)


def attend(query_units, key_units, value_units, resid_units, doc_units):
    head = query_units.shape[2]
    scores = jnp.einsum(
        "uqd,ukd->uqk", query_units, key_units, preferred_element_type=F32
    ) / math.sqrt(head)
    positions = jnp.arange(query_units.shape[1], dtype=jnp.int32)
    distance = positions[:, None] - positions[None, :]
    allowed = (doc_units[:, :, None] == doc_units[:, None, :]) & (
        (distance >= 0) & (distance < WIN)
    )[None]
    scores = jnp.where(allowed, scores, -1e30)
    row_max = jnp.max(scores, axis=2, keepdims=True)
    exp_scores = jnp.exp(scores - row_max)
    attn_probs = (exp_scores / jnp.sum(exp_scores, axis=2, keepdims=True)).astype(BF16)
    mixed = jnp.einsum("uqk,ukd->uqd", attn_probs, value_units, preferred_element_type=F32)
    return (resid_units.astype(F32) + mixed).astype(BF16)


def column_parts(full, width):
    x, c = lax.axis_index("x"), lax.axis_index("c")
    n = lax.axis_size("x")
    block = lambda s, core: part_of(full, 2 * ((x + s) % n) + core, width, 1)
    return (block(0, c), block(0, 1 - c)), (block(1, c), block(n - 1, c), block(2, c))


def columns_over_x(to_send):
    up, down, far = to_send
    return moved(down, "x", -1), moved(up, "x", 1), moved(far, "x", 2)


def column_blocks(own, arrived, other):
    mine = jnp.concatenate([own[0], *arrived], axis=0)
    theirs = jnp.concatenate([own[1], other[0], other[1], other[2]], axis=0)
    same = lax.axis_index("c") == lax.axis_index("yh")
    return jnp.where(same, mine, theirs), jnp.where(same, theirs, mine)


def near_over_x(factor):
    return moved(factor, "x", 1), moved(factor, "x", -1)


def far_over_x(near):
    below, above = near
    half = below.shape[0] // 2
    return moved(below[:half], "x", 1), moved(above[half:], "x", -1)


def all_over_x(factor, near, far):
    below, above = near
    return jnp.concatenate([factor, above, below, jnp.concatenate(far, axis=0)], axis=1)


def shared_part(factor_all, send):
    return jnp.dot(factor_all, send, preferred_element_type=F32).astype(BF16)


class RowSums:
    def __init__(self, parts, rows_here):
        self.rows_here = rows_here
        self.c, self.z = lax.axis_index("c"), lax.axis_index("z")
        self.yl = lax.axis_index("yl")
        self.n = lax.axis_size("z")
        half = parts[0].shape[1] // 2
        shape = (2, self.n, 2 * rows_here, half)
        self.pairs = []
        for part in parts:
            arrived = moved(part_of(part, 1 - self.c, half, 1), "c", 1)
            kept = part_of(part, self.c, half, 1)
            self.pairs += [(kept.reshape(shape), arrived.reshape(shape))]

    def own(self, r):
        at = (self.z + r) % self.n
        pick = lambda a: lax.dynamic_slice_in_dim(a, at, 1, 1)[:, 0].astype(F32)
        return jnp.stack([pick(kept) + pick(arrived) for kept, arrived in self.pairs], axis=1)

    def first(self):
        far = self.own(self.n // 2).astype(BF16)
        return far[0], far[1]

    def second(self, up, down):
        near = self.own(self.n // 2 - 1)
        above = jnp.stack([near[0] + up.astype(F32), near[1]])
        near = self.own(self.n - self.n // 2 + 1)
        below = jnp.stack([near[0], near[1] + down.astype(F32)])
        return above.astype(BF16), below.astype(BF16)

    def later(self, r, up, down):
        up = self.own(r) + up.astype(F32)
        down = self.own(self.n - r) + down.astype(F32)
        return up.astype(BF16), down.astype(BF16)

    def sent(self, pair):
        return moved(pair[0], "z", 1), moved(pair[1], "z", -1)

    def last(self, up, down):
        total = self.own(0) + up.astype(F32) + down.astype(F32)
        mine = lax.dynamic_index_in_dim(total, self.yl, 0, keepdims=False)
        other = lax.dynamic_index_in_dim(total, 1 - self.yl, 0, keepdims=False)
        pair = moved(other.astype(BF16), "yl", 1)
        both = mine + pair.astype(F32)
        rows = part_of(both, self.c, self.rows_here, 1)
        return rows, moved(part_of(both, 1 - self.c, self.rows_here, 1), "c", 1)


def together(*values):
    return lax.optimization_barrier(values)


def whole_step(
    query_states,
    key_states,
    value_states,
    residual,
    norm_gains,
    lang_labels,
    doc_lengths,
    destinations,
    gate_weight,
    up_weight,
    down_weight,
    out_cotangent,
):
    groups = lax.axis_size(DP)
    my_group = lax.axis_index(DP)
    c, yl = lax.axis_index("c"), lax.axis_index("yl")
    total_units = destinations.shape[0]
    per_group = total_units // groups
    columns = query_states.shape[1]
    width = gate_weight.shape[0]
    tok_group = per_group * UNIT
    rows_here = out_cotangent.shape[0]
    half = width // 2
    gate_t = gate_weight.T
    up_t = up_weight.T

    pair_rows = moved(part_of(out_cotangent, 1 - c, half, 1), "c", 1)
    chip_rows = joined(part_of(out_cotangent, c, half, 1), pair_rows, c, 0)
    run_rows = sent_over_z(chip_rows).reshape(-1, half)
    doc_ids = doc_index(doc_lengths, UNIT)
    unit_index = jnp.arange(total_units, dtype=jnp.int32)
    earlier = unit_index[None, :] < unit_index[:, None]
    same_target = destinations[None, :] == destinations[:, None]
    arrival = jnp.sum((earlier & same_target).astype(jnp.int32), axis=1)
    first_unit = my_group * per_group
    landing_at = jnp.where(destinations == my_group, arrival, -1)
    arrive_ids = jnp.arange(per_group, dtype=jnp.int32)
    landing = landing_at[None, :] == arrive_ids[:, None]
    moved_langs = jnp.sum(landing.astype(jnp.int32) * lang_labels[None, :], axis=1)
    near_x = (lax.axis_index("x") + jnp.arange(groups // 2, dtype=jnp.int32)) % (groups // 2)
    near_y = (lax.axis_index("yh") + jnp.arange(2, dtype=jnp.int32)) % 2
    held_group = (near_x[:, None] * 2 + near_y[None, :]).reshape(-1)
    held_unit = (held_group[:, None] * per_group + arrive_ids[None, :]).reshape(-1)
    held_at = jnp.sum(
        jnp.where(held_unit[:, None] == unit_index[None, :], landing_at[None, :], 0), axis=1
    )
    pick_table = (held_at[None, :] == arrive_ids[:, None]).astype(BF16)
    unit_shape = (per_group, UNIT, columns)
    own_docs = lax.dynamic_slice_in_dim(doc_ids, first_unit, per_group, 0)
    local_mix = attend(
        query_states.reshape(unit_shape),
        key_states.reshape(unit_shape),
        value_states.reshape(unit_shape),
        residual.reshape(unit_shape),
        own_docs,
    )
    pair_mix = jnp.concatenate([local_mix, moved(local_mix, "yh", 1)], axis=0)
    others = [moved(pair_mix, "x", step) for step in (-1, 2, 1)]
    held = jnp.concatenate([pair_mix, *others], axis=0)
    stream_cols = (
        jnp.einsum("ju,uic->jic", pick_table, held, preferred_element_type=F32)
        .astype(BF16)
        .reshape(tok_group, columns)
    )

    langs = jnp.arange(norm_gains.shape[0], dtype=jnp.int32)
    unit_gain = jnp.sum(
        jnp.where((moved_langs[:, None] == langs[None, :])[:, :, None], norm_gains[None], 0.0),
        axis=1,
    )
    both_yl = joined(stream_cols[None], moved(stream_cols, "yl", 1)[None], yl, 0)
    run_cols = ring_over_z(both_yl)
    pair_rows = moved(run_rows, "yl", 1)
    cot_half = joined(run_rows, pair_rows, yl, 0)
    pair_half = moved(cot_half, "c", 1)
    cot_full = joined(cot_half, pair_half, c, 1)
    cot_own, cot_send = column_parts(cot_full, width // groups)
    cot_arrived = columns_over_x(cot_send)
    nt = (((1,), (1,)), ((), ()))
    tn = (((0,), (0,)), ((), ()))
    grad_hidden = lax.dot_general(down_weight, cot_full, nt, preferred_element_type=F32)
    other_cols = moved(run_cols, "c", 1)
    stream, scaled, squares = assembled(run_cols, other_cols, unit_gain)
    scaled_own, scaled_send = column_parts(scaled, width // groups)
    scaled_arrived = columns_over_x(scaled_send)
    inv_rms = lax.rsqrt(jnp.sum(squares, axis=1) / width + 1e-05)
    gate_acc = lax.dot_general(gate_t, scaled, nt, preferred_element_type=F32)
    up_acc = lax.dot_general(up_t, scaled, nt, preferred_element_type=F32)
    rms_row = inv_rms[None, :]
    act_gate = rms_row * gate_acc
    act_up = rms_row * up_acc
    sigma = jax.nn.sigmoid(act_gate)
    silu = act_gate * sigma
    hidden = (silu * act_up).astype(BF16)
    scaled_grad = rms_row * grad_hidden
    grad_gate = (scaled_grad * act_up * sigma * (1.0 + act_gate * (1.0 - sigma))).astype(BF16)
    grad_up = (scaled_grad * silu).astype(BF16)
    gate_up = jnp.concatenate([grad_gate, grad_up], axis=0)

    near_hidden = near_over_x(hidden)
    near_gate_up = near_over_x(gate_up)
    out_part = lax.dot_general(hidden, down_weight, tn, preferred_element_type=F32).astype(
        BF16
    )
    back_part = (
        lax.dot_general(grad_gate, gate_t, tn, preferred_element_type=F32)
        + lax.dot_general(grad_up, up_t, tn, preferred_element_type=F32)
    ).astype(BF16)
    sums = RowSums([out_part, back_part], rows_here)
    ring = sums.first()
    ring = sums.sent(ring)
    ring = sums.second(*ring)
    ring = sums.sent(ring)
    far_gate_up = far_over_x(near_gate_up)
    far_hidden = far_over_x(near_hidden)
    scaled_other = moved(jnp.stack(scaled_arrived), "c", 1)
    cot_other = moved(jnp.stack(cot_arrived), "c", 1)
    ring = sums.later(2, *ring)
    ring = sums.sent(ring)
    scaled_keep, scaled_share = column_blocks(scaled_own, scaled_arrived, scaled_other)
    cot_keep, cot_share = column_blocks(cot_own, cot_arrived, cot_other)
    gate_up_all = all_over_x(gate_up, near_gate_up, far_gate_up)
    hidden_all = all_over_x(hidden, near_hidden, far_hidden)
    hidden_sent = shared_part(hidden_all, cot_share)
    hidden_share = moved(hidden_sent, "yh", 1)
    gate_up_sent = shared_part(gate_up_all, scaled_share)
    gate_up_share = moved(gate_up_sent, "yh", 1)
    ring = sums.later(1, *ring)
    ring = sums.sent(ring)
    gate_up_kept = jnp.dot(gate_up_all, scaled_keep, preferred_element_type=F32)
    hidden_kept = jnp.dot(hidden_all, cot_keep, preferred_element_type=F32)
    gate_up_kept, hidden_kept = together(gate_up_kept, hidden_kept)
    sums, pair_sums = sums.last(*ring)
    gate_up_grad = (gate_up_kept + gate_up_share.astype(F32)).astype(BF16)
    down_grad = (hidden_kept + hidden_share.astype(F32)).astype(BF16)
    hidden_here = gate_weight.shape[1]
    gate_grad = gate_up_grad[:hidden_here].T
    up_grad = gate_up_grad[hidden_here:].T
    layer_out, input_grad = finished(sums, pair_sums, stream, unit_gain, out_cotangent)
    return (layer_out, input_grad, gate_grad, up_grad, down_grad)


def solution(mesh):
    finer = Mesh(mesh.devices.reshape(mesh.shape["dp"] // 2, 2, 2, -1, 2), DP_TENSOR)
    head_cols = P(DP, TENSOR)
    return jax.shard_map(
        whole_step,
        mesh=finer,
        in_specs=(
            head_cols,
            head_cols,
            head_cols,
            head_cols,
            P(),
            P(),
            P(),
            P(),
            P(None, TENSOR),
            P(None, TENSOR),
            P(TENSOR, None),
            P(DP_TENSOR, None),
        ),
        out_specs=(
            P(DP_TENSOR, None),
            P(DP_TENSOR, None),
            P(DP, TENSOR),
            P(DP, TENSOR),
            P(TENSOR, DP),
        ),
        check_vma=False,
    )
```
